256 devices in a mesh: art: 64 (over z, y, core), seq: 4 (over x).
Axes of the slice: x: 4, y: 4, z: 8, core: 2. Of those that a mesh axis runs over, the one named last changes fastest.
Arguments:
- queries: bfloat16 [768, 4, 256, 128], P('art', 'seq'), may hold values from -6 to 6
- cand_owner: int32 [3072, 16, 4], P(('art', 'seq')), may hold values from 0 to 63, all different within a row; in each aligned block of 192 rows (0 to 191, 192 to 383, ..., all dimensions but the last counted through in order) at most 18 rows name the same one
- cand_local: int32 [3072, 16, 4], P(('art', 'seq')), may hold values from 0 to 255, as said below
- companies: bfloat16 [16384, 64, 128], P('art'), may hold values from -6 to 6
Outputs:
- relevance: float32 [3072, 64], P(('art', 'seq'))
- probs: float32 [3072, 64], P(('art', 'seq'))
The draws below stay inside these ranges and needn't reach their ends.
Inputs may be any that keep to these rules, and one draw needn't show every extreme that they name: `cand_owner`: each row of four candidates names four different owners. Among the candidates of one device's 12 articles (aligned blocks of 12 articles in the order of the array), no owner is named more than 18 times, a bound that some block reaches. `cand_local`: the candidates of one device's 12 articles (aligned blocks of 12 articles in the order of the array) name exactly 9 different local indices in all.
All inputs are finite; a program needn't handle non-finite values.
Results may differ from the reference program's by a relative error of at most 0.0088.
Values may be sent and summed in bfloat16 or wider, within the bound.
A program may use at most 128 MiB of HBM per device.

```python
import math
import jax
import jax.numpy as jnp
import numpy as np
from jax import lax

E = 128
LQ = 256
LC = 64
NC = 64
A_DEV = 12
C_DEV = 256
CAP = 18
DIST = 9
ARTICLES = 3072
COMPANIES = 16384
N_ART = 64
N_SEQ = 4


def draw_cand_local(key, part):
    block_count = ARTICLES // A_DEV
    per_block = A_DEV * NC
    stride = C_DEV // DIST
    keys = jax.random.split(key, block_count + 1)
    spread = jax.random.randint(keys[0], (block_count,), 0, C_DEV)
    base = spread * spread // C_DEV
    base = base.at[0].set(C_DEV - 1).at[1].set(0)
    order = jax.vmap(lambda k: jax.random.permutation(k, per_block))(keys[1:]) % DIST
    local = (base[:, None] + order * stride) % C_DEV
    return local.reshape(ARTICLES, NC // 4, 4).astype(jnp.int32)


def shard_levels(own_key, extent, cuts, low, top_value):
    def one(dim, shards_of):
        steps = jax.random.uniform(jax.random.fold_in(jax.random.fold_in(own_key, 6), dim), (shards_of,), jnp.float32, low / len(cuts), top_value / len(cuts))
        return jnp.repeat(jnp.exp(steps), extent[dim] // shards_of).reshape((-1,) + (1,) * (len(extent) - dim - 1))

    level = one(*cuts[0])
    for cut in cuts[1:]:
        level = level * one(*cut)
    return level


def assign_block(own_key, own, number, rows, number_of, top, bound, skew):
    sequence = jax.random.permutation(own_key, number_of)
    crowded, ordinary = portions_of(number_of, rows * top, bound, skew, True), portions_of(number_of, rows * top, bound, skew, False)
    places = jnp.arange(number_of)

    def named(tallies, rotation):
        used = int((tallies > 0).sum())
        fixed = max(1, used // 4)
        passed = fixed + (places - fixed + rotation * (used - fixed)) % max(1, number_of - fixed)
        return jnp.zeros((number_of,), jnp.int32).at[sequence[jnp.where(places < fixed, places, passed)]].set(jnp.asarray(tallies, jnp.int32))

    tallies = jnp.where(number % 4 == 0, named(crowded, number // 4), named(ordinary, number - number // 4 - 1))
    mixed = jax.random.permutation(jax.random.fold_in(own, 3), number_of)
    giver, taker = mixed[0:number_of // 2 * 2:2], mixed[1:number_of // 2 * 2:2]
    margin = jnp.minimum(tallies[giver] - 1, bound - tallies[taker]) // 2
    margin = jnp.where((giver == sequence[0]) | (taker == sequence[0]) | (tallies[taker] == 0), 0, jnp.maximum(margin, 0))
    passed = jax.random.randint(jax.random.fold_in(own, 4), (number_of // 2,), 0, 1 << 20) % (margin + 1)
    tallies = tallies.at[giver].add(-passed).at[taker].add(passed)
    items = jnp.searchsorted(jnp.cumsum(tallies), jnp.arange(rows * top), side="right").astype(jnp.int32)
    grid = items.reshape(top, rows).T
    grid = grid[jax.random.permutation(jax.random.fold_in(own, 1), rows)]
    rotation = jax.random.randint(jax.random.fold_in(own, 2), (rows, 1), 0, top)
    return jnp.take_along_axis(grid, (jnp.arange(top)[None, :] + rotation) % top, axis=1)


def portions_of(amount, total, most, lean, full):
    loads = [(1 << 20) // math.isqrt(grade ** lean) + 1 for grade in range(1, amount + 1)]
    largest = most if full else min(most, max(-(-total // amount), total * loads[0] // sum(loads)))
    least = 1 if total - largest >= amount - 1 else 0
    given, rest = [largest] + [least] * (amount - 1), total - largest - least * (amount - 1)
    while rest > 0:
        free = [i for i in range(1, amount) if given[i] < largest] or [i for i in range(1, amount) if given[i] < most]
        pool, remaining = sum([loads[i] for i in free]), rest
        for i in free:
            extra = min(most - given[i], max(1, remaining * loads[i] // pool), rest)
            given[i] = given[i] + extra
            rest = rest - extra
    return np.array(given)


def scatter_about(key, extent, deviation, reach, cuts=(), held_as=jnp.bfloat16):
    loudness = shard_levels(key, extent, cuts, -0.22, 0.18) if cuts else 1.0
    array = jax.random.normal(key, extent, jnp.float32) * deviation * loudness
    return jnp.minimum(jnp.maximum(array, -reach), reach).astype(held_as)


def setup_inputs(seed: int = 0) -> dict:
    streams_of = jax.random.split(jax.random.key(seed), 5)
    queries = scatter_about(streams_of[0], (ARTICLES // N_SEQ, N_SEQ, LQ, E), 1.0, 6.0, ((0, 64), (1, 4)))
    cand_owner_keys = jax.random.split(jax.random.fold_in(streams_of[1], 1), ARTICLES * (NC // 4) // (A_DEV * NC // 4))
    cand_owner_turns = jax.random.permutation(jax.random.fold_in(streams_of[1], 3), ARTICLES * (NC // 4) // (A_DEV * NC // 4))
    cand_owner = jax.vmap(lambda own, number: assign_block(jax.random.fold_in(streams_of[1], 2), own, number, A_DEV * NC // 4, N_ART, 4, CAP, 2))(cand_owner_keys, cand_owner_turns).reshape((ARTICLES, NC // 4, 4))
    cand_local = draw_cand_local(jax.random.fold_in(streams_of[4], 71), 0)
    companies = scatter_about(streams_of[3], (COMPANIES, LC, E), 1.0, 6.0, ((0, 64),))
    return dict(queries=queries, cand_owner=cand_owner, cand_local=cand_local, companies=companies)


EPS = 1e-06
SHARP = 16.0
TEMPER = 4.0

def unit_rows(values):
    wide = values.astype(jnp.float32)
    return (wide * lax.rsqrt(lax.optimization_barrier(jnp.sum(wide * wide, axis=-1, keepdims=True)) + EPS)).astype(jnp.bfloat16)

def reference(queries, cand_owner, cand_local, companies):
    query_unit = unit_rows(queries.reshape(ARTICLES, LQ, E))
    company_unit = unit_rows(companies)
    cand_id = (cand_owner * C_DEV + cand_local).reshape(ARTICLES, NC).astype(jnp.int32)

    def one_article(pair):
        query_rows, ids = pair
        blocks = company_unit[ids].reshape(NC * LC, E)
        sims = jnp.dot(query_rows.astype(jnp.float32), blocks.astype(jnp.float32).T, preferred_element_type=jnp.float32)
        mass = lax.optimization_barrier(jnp.sum(jnp.exp(sims * SHARP).reshape(LQ, NC, LC), axis=-1))
        return lax.optimization_barrier(jnp.sum(jnp.log(mass), axis=0)) / SHARP
    score = lax.map(one_article, (query_unit, cand_id))
    relevance = score - lax.optimization_barrier(jnp.mean(score, axis=-1, keepdims=True))
    weights = jnp.exp(TEMPER * relevance)
    probs = weights / lax.optimization_barrier(jnp.sum(weights, axis=-1, keepdims=True))
    return (relevance, probs)
```

```python
import math

import jax
import jax.numpy as jnp
from jax import lax
from jax.experimental import pallas as pl
from jax.experimental.pallas import tpu as pltpu
from jax.sharding import PartitionSpec as P

EPS = 1e-06
SHARP = 16.0
TEMPER = 4.0
MESH = pl.DeviceIdType.MESH
HBM = pl.BlockSpec(memory_space=pl.ANY)
VMEM = pl.BlockSpec(memory_space=pltpu.VMEM)

NX, NY, NZ = 4, 4, 8
ARTS = 12
PART = ARTS // NX
LQ, LC, E = 256, 64, 128
NC = 64
C_DEV = 256
CAP = 18
SLOTS = NY * CAP
GROUPS = SLOTS // 8
WORKERS = NZ * 2
REQ = ARTS * NC
SPLIT = 160
QUARTER = SPLIT // NX
HALF = QUARTER // 2
REST = (C_DEV - SPLIT) // 2


def unit(values):
    wide = values.astype(jnp.float32)
    return wide * lax.rsqrt(jnp.sum(wide * wide, axis=-1, keepdims=True) + EPS)


def place():
    art, x = lax.axis_index("art"), lax.axis_index("seq")
    return art // (NY * 2), (art // 2) % NY, art % 2, x


def prepare_kernel(own_ref, loc_ref, q_ref, c_ref, qt_ref, cat_ref, list_ref, slot_ref):
    def normalise(i, carry):
        cat_ref[pl.ds(i * 8, 8)] = unit(c_ref[pl.ds(i * 8, 8)]).astype(jnp.bfloat16)
        return carry

    lax.fori_loop(0, c_ref.shape[0] // 8, normalise, 0)
    for a in range(PART):
        qt_ref[a] = jnp.transpose(unit(q_ref[a])).astype(jnp.bfloat16)

    @pl.when(pl.program_id(0) == 0)
    def _():
        z, y, c, x = place()
        owner = own_ref[...]
        local = loc_ref[...]
        oz, oy, oc = owner // (NY * 2), (owner // 2) % NY, owner % 2
        lane = lax.broadcasted_iota(jnp.int32, (REQ, 128), 1)
        row = lax.broadcasted_iota(jnp.int32, (REQ, 1), 0)
        hot = lane == (oz * 2 + oc) * NY + oy
        table = jnp.where(hot, 1.0, 0.0).astype(jnp.bfloat16)
        first = lax.broadcasted_iota(jnp.int32, (REQ, REQ), 0)
        second = lax.broadcasted_iota(jnp.int32, (REQ, REQ), 1)
        before = jnp.where(second < first, 1.0, 0.0).astype(jnp.bfloat16)
        counts = jnp.dot(before, table, preferred_element_type=jnp.float32)
        rank = jnp.sum(jnp.where(hot, counts, 0.0), axis=1, keepdims=True).astype(jnp.int32)
        article = row // NC
        held = article % NX
        spot = ((x - held + NX) % NX) * PART + article // NX
        value = jnp.where(lane < 64, spot, local)
        entry = jnp.where(lane % 64 == rank, value, 0).astype(jnp.float32).astype(jnp.bfloat16)
        lists = lax.dot_general(
            table, entry, (((0,), (0,)), ((), ())), preferred_element_type=jnp.float32
        )
        lists = lists[: WORKERS * NY].astype(jnp.int32)
        for w in range(WORKERS):
            list_ref[w, 0:NY] = lists[w * NY : (w + 1) * NY]
            list_ref[w, NY:8] = jnp.zeros((8 - NY, 128), jnp.int32)
        pos = oy * CAP + rank
        side = ((z - oz + NZ) % NZ) * 2 + jnp.where(oc == c, 0, 1)
        slot_ref[...] = jnp.where(lane < 64, side * 8 + pos % 8, pos // 8)


def prepare(owners, locals_, queries, companies):
    steps = NX
    blocks = C_DEV // steps
    return pl.pallas_call(
        prepare_kernel,
        grid=(steps,),
        out_shape=(
            jax.ShapeDtypeStruct((ARTS, E, LQ), jnp.bfloat16),
            jax.ShapeDtypeStruct((C_DEV, LC, E), jnp.bfloat16),
            jax.ShapeDtypeStruct((WORKERS, 8, 128), jnp.int32),
            jax.ShapeDtypeStruct((REQ, 128), jnp.int32),
        ),
        in_specs=[
            pl.BlockSpec((REQ, 1), lambda i: (0, 0)),
            pl.BlockSpec((REQ, 1), lambda i: (0, 0)),
            pl.BlockSpec((PART, LQ, E), lambda i: (i, 0, 0)),
            pl.BlockSpec((blocks, LC, E), lambda i: (i, 0, 0)),
        ],
        out_specs=(
            pl.BlockSpec((PART, E, LQ), lambda i: (i, 0, 0)),
            pl.BlockSpec((blocks, LC, E), lambda i: (i, 0, 0)),
            pl.BlockSpec((WORKERS, 8, 128), lambda i: (0, 0, 0)),
            pl.BlockSpec((REQ, 128), lambda i: (0, 0)),
        ),
    )(owners, locals_, queries, companies)


N_COPIES = 96


def spread_kernel(qt_ref, cat_ref, list_ref, qall_ref, slab_ref, lrecv_ref, send_sem, recv_sem, local_sem):
    z, y, c, x = place()

    def at(dz=0, dy=0, dc=0, dx=0):
        zz, yy, cc, xx = (z + dz + NZ) % NZ, (y + dy + NY) % NY, (c + dc) % 2, (x + dx + NX) % NX
        return ((zz * NY + yy) * 2 + cc, xx)

    peers = [at(dz=-d, dc=k) for d in range(NZ) for k in range(2) if d or k]
    peers += [at(dy=1), at(dy=-1), at(dx=1), at(dx=2), at(dx=3)]
    barrier = pltpu.get_barrier_semaphore()
    for peer in peers:
        pl.semaphore_signal(barrier, inc=1, device_id=peer, device_id_type=MESH)
    pl.semaphore_wait(barrier, len(peers))

    copies = {}

    def send(name, src, dst, device):
        assert name not in copies
        n = len(copies)
        copy = pltpu.make_async_remote_copy(
            src_ref=src,
            dst_ref=dst,
            send_sem=send_sem.at[n],
            recv_sem=recv_sem.at[n],
            device_id=device,
            device_id_type=MESH,
        )
        copies[name] = copy
        copy.start()

    received = set()

    def got(*names):
        for name in names:
            if name not in received:
                received.add(name)
                copies[name].wait_recv()

    own_list = pltpu.make_async_copy(list_ref.at[z * 2 + c], lrecv_ref.at[0], local_sem.at[0])
    own_list.start()
    for d in range(NZ):
        for k in range(2):
            if d or k:
                worker = ((z - d + NZ) % NZ) * 2 + (c + k) % 2
                send(f"l{d}{k}", list_ref.at[worker], lrecv_ref.at[d * 2 + k], at(dz=-d, dc=k))

    own_part = pltpu.make_async_copy(
        qt_ref.at[pl.ds(x * PART, PART)], qall_ref.at[0, 0, pl.ds(0, PART)], local_sem.at[1]
    )
    own_part.start()
    for j in (1, 3, 2):
        send(
            f"e{j}",
            qt_ref.at[pl.ds(((x + j) % NX) * PART, PART)],
            qall_ref.at[0, 0, pl.ds(j * PART, PART)],
            at(dx=j),
        )

    def z_first(j):
        rows = pl.ds(j * PART, PART)
        src = qt_ref.at[pl.ds(x * PART, PART)] if j == 0 else qall_ref.at[0, 0, rows]
        send(f"p1{j}", src, qall_ref.at[NZ - 1, 0, rows], at(dz=1))
        send(f"m1{j}", src, qall_ref.at[1, 0, rows], at(dz=-1))

    def z_next(step, half, both=(True, True)):
        rows = pl.ds(half * 2 * PART, 2 * PART)
        if both[0]:
            send(f"p{step}{half}", qall_ref.at[NZ - step + 1, 0, rows], qall_ref.at[NZ - step, 0, rows], at(dz=1))
        if both[1]:
            send(f"m{step}{half}", qall_ref.at[step - 1, 0, rows], qall_ref.at[step, 0, rows], at(dz=-1))

    def partner(dz):
        send(f"c{dz}", qall_ref.at[dz, 0], qall_ref.at[dz, 1], at(dc=1))

    def quarter(of, h):
        return pl.ds(((x + of + NX) % NX) * QUARTER + h * HALF, HALF)

    def rest(h):
        return pl.ds(SPLIT + h * REST, REST)

    def y_own(tag, rows, h):
        def up():
            send(f"up{tag}{h}", cat_ref.at[rows(h)], slab_ref.at[2, rows(h)], at(dy=1))

        def down():
            send(f"dn{tag}{h}", cat_ref.at[rows(h)], slab_ref.at[0, rows(h)], at(dy=-1))

        return up, down

    def y_fwd(tag, rows):
        send(f"up2{tag}", slab_ref.at[2, rows(0)], slab_ref.at[1, rows(0)], at(dy=1))
        send(f"dn2{tag}", slab_ref.at[0, rows(1)], slab_ref.at[1, rows(1)], at(dy=-1))

    def x_own(d, h):
        rows = quarter(0, h)
        send(f"xp{d}{h}", slab_ref.at[d, rows], slab_ref.at[d, rows], at(dx=1))
        send(f"xm{d}{h}", slab_ref.at[d, rows], slab_ref.at[d, rows], at(dx=-1))

    def x_fwd(d):
        got(f"xp{d}0")
        rows = quarter(-1, 0)
        send(f"xpf{d}", slab_ref.at[d, rows], slab_ref.at[d, rows], at(dx=1))
        got(f"xm{d}1")
        rows = quarter(1, 1)
        send(f"xmf{d}", slab_ref.at[d, rows], slab_ref.at[d, rows], at(dx=-1))

    mine = lambda h: quarter(0, h)
    y_own("s", mine, 0)[0]()
    y_own("s", mine, 1)[1]()
    y_own("s", mine, 1)[0]()
    y_own("s", mine, 0)[1]()
    z_first(0)
    got("e1")
    z_first(1)
    got("e3")
    z_first(3)
    got("ups0", "dns1")
    y_fwd("s", mine)
    for h in (0, 1):
        y_own("r", rest, h)[0]()
        y_own("r", rest, 1 - h)[1]()
    x_own(2, 0)
    x_own(0, 1)
    got("e2")
    z_first(2)
    own_part.wait()
    partner(0)
    got("p10", "p11", "m10", "m11")
    z_next(2, 0)
    got("ups1", "dns0")
    x_own(2, 1)
    x_own(0, 0)
    got("p12", "p13", "m12", "m13")
    z_next(2, 1)
    partner(NZ - 1)
    partner(1)
    got("up2s", "dn2s")
    x_own(1, 0)
    x_own(1, 1)
    got("p20", "m20")
    z_next(3, 0)
    x_fwd(2)
    x_fwd(0)
    got("p21", "m21")
    z_next(3, 1)
    partner(NZ - 2)
    partner(2)
    got("upr0", "dnr1")
    y_fwd("r", rest)
    got("p30")
    z_next(4, 0, (True, False))
    got("m30", "m31")
    z_next(4, 1, (False, True))
    got("p31")
    partner(NZ - 3)
    partner(3)
    x_fwd(1)
    got("p40", "m41")
    partner(4)
    own_list.wait()
    for name in list(copies):
        got(name)
    for copy in copies.values():
        copy.wait_send()


def spread(qt, cat, lists):
    return pl.pallas_call(
        spread_kernel,
        out_shape=(
            jax.ShapeDtypeStruct((NZ, 2, ARTS, E, LQ), jnp.bfloat16),
            jax.ShapeDtypeStruct((NY - 1, C_DEV, LC, E), jnp.bfloat16),
            jax.ShapeDtypeStruct((WORKERS, 8, 128), jnp.int32),
        ),
        in_specs=[HBM, HBM, HBM],
        out_specs=(HBM, HBM, HBM),
        scratch_shapes=[
            pltpu.SemaphoreType.DMA((N_COPIES,)),
            pltpu.SemaphoreType.DMA((N_COPIES,)),
            pltpu.SemaphoreType.DMA((2,)),
        ],
        compiler_params=pltpu.CompilerParams(collective_id=0, has_side_effects=True),
    )(qt, cat, lists)


def pool_kernel(list_ref, q_hbm, own_hbm, slab_hbm, out_ref, q_ref, cat_ref, q_sem, c_sem):
    z, y, c, x = place()
    loads = [pltpu.make_async_copy(own_hbm, cat_ref.at[y], c_sem.at[0])]
    for d in range(1, NY):
        loads.append(pltpu.make_async_copy(slab_hbm.at[d - 1], cat_ref.at[(y + d) % NY], c_sem.at[d]))

    def q_load(w):
        return pltpu.make_async_copy(q_hbm.at[w // 2, w % 2], q_ref.at[w], q_sem.at[w])

    q_load(0).start()
    for load in loads:
        load.start()
    for w in range(1, WORKERS):
        q_load(w).start()
    for load in loads:
        load.wait()
    lane = lax.broadcasted_iota(jnp.int32, (8, 128), 1)

    def source(w, carry):
        q_load(w).wait()
        scores = jnp.zeros((8, 128), jnp.float32)
        for g in range(GROUPS):
            rows = []
            for u in range(8):
                owner, slot = divmod(g * 8 + u, CAP)
                query = q_ref[w, list_ref[w, owner, slot]]
                block = cat_ref[owner, list_ref[w, owner, 64 + slot]]
                sims = jnp.dot(block, query, preferred_element_type=jnp.float32)
                mass = jnp.exp2(sims * (SHARP * math.log2(math.e)))
                rows.append(jnp.sum(jnp.sum(mass.reshape(8, 8, LQ), axis=0), axis=0, keepdims=True))
            logs = jnp.log(jnp.concatenate(rows, axis=0))
            scores = jnp.where(lane == g, jnp.sum(logs, axis=1, keepdims=True) * (1.0 / SHARP), scores)
        out_ref[w] = scores
        return carry

    lax.fori_loop(0, WORKERS, source, 0)


def pool(lists, qall, cat, slab):
    return pl.pallas_call(
        pool_kernel,
        out_shape=jax.ShapeDtypeStruct((WORKERS, 8, 128), jnp.float32),
        in_specs=[pl.BlockSpec(memory_space=pltpu.SMEM), HBM, HBM, HBM],
        out_specs=VMEM,
        scratch_shapes=[
            pltpu.VMEM((WORKERS, ARTS, E, LQ), jnp.bfloat16),
            pltpu.VMEM((NY, C_DEV, LC, E), jnp.bfloat16),
            pltpu.SemaphoreType.DMA((WORKERS,)),
            pltpu.SemaphoreType.DMA((NY,)),
        ],
        compiler_params=pltpu.CompilerParams(vmem_limit_bytes=56 << 20),
    )(lists, qall, cat, slab)


def finish_kernel(part_ref, slot_ref, rel_ref, prob_ref, recv_ref, send_sem, recv_sem, local_sem):
    z, y, c, x = place()

    def at(dz, dc):
        return ((((z + dz + NZ) % NZ) * NY + y) * 2 + (c + dc) % 2, x)

    pairs = [(d, k) for d in range(NZ) for k in range(2) if d or k]
    barrier = pltpu.get_barrier_semaphore()
    for d, k in pairs:
        pl.semaphore_signal(barrier, inc=1, device_id=at(d, k), device_id_type=MESH)
    pl.semaphore_wait(barrier, len(pairs))
    own = pltpu.make_async_copy(part_ref.at[0], recv_ref.at[0], local_sem)
    own.start()
    copies = []
    for d, k in pairs:
        n = d * 2 + k
        copies.append(
            pltpu.make_async_remote_copy(
                src_ref=part_ref.at[n],
                dst_ref=recv_ref.at[n],
                send_sem=send_sem.at[n],
                recv_sem=recv_sem.at[n],
                device_id=at(d, k),
                device_id_type=MESH,
            )
        )
        copies[-1].start()
    lane = lax.broadcasted_iota(jnp.int32, (REQ, 128), 1)
    slots = slot_ref[...]
    hot_row = jnp.where(lane == slots[:, 0:1], 1.0, 0.0).astype(jnp.bfloat16)
    hot_lane = lane == slots[:, 64:65]
    own.wait()
    for copy in copies:
        copy.wait()
    values = recv_ref[...].reshape(128, 128)
    picked = jnp.zeros((REQ, 128), jnp.float32)
    for _ in range(3):
        head = values.astype(jnp.bfloat16)
        picked = picked + jnp.dot(hot_row, head, preferred_element_type=jnp.float32)
        values = values - head.astype(jnp.float32)
    score = jnp.sum(jnp.where(hot_lane, picked, 0.0), axis=1, keepdims=True)
    wide = lax.broadcasted_iota(jnp.int32, (NC, 128), 1)
    columns = jnp.zeros((NC, 128), jnp.float32)
    for a in range(ARTS):
        columns = jnp.where(wide == a, score[a * NC : (a + 1) * NC], columns)
    relevance = columns - jnp.sum(columns, axis=0, keepdims=True) * (1.0 / NC)
    weights = jnp.exp(TEMPER * relevance)
    probs = weights / jnp.sum(weights, axis=0, keepdims=True)
    both = jnp.transpose(jnp.concatenate([relevance, probs], axis=0))
    rel_ref[...] = both[0:ARTS, 0:NC]
    prob_ref[...] = both[0:ARTS, NC:]


def finish(part, slots):
    return pl.pallas_call(
        finish_kernel,
        out_shape=(jax.ShapeDtypeStruct((ARTS, NC), jnp.float32),) * 2,
        in_specs=[HBM, VMEM],
        out_specs=(VMEM, VMEM),
        scratch_shapes=[
            pltpu.VMEM((WORKERS, 8, 128), jnp.float32),
            pltpu.SemaphoreType.DMA((WORKERS,)),
            pltpu.SemaphoreType.DMA((WORKERS,)),
            pltpu.SemaphoreType.DMA,
        ],
        compiler_params=pltpu.CompilerParams(collective_id=1, has_side_effects=True),
    )(part, slots)


def per_device(queries, cand_owner, cand_local, companies):
    held = queries.reshape(ARTS, LQ, E)
    qt, cat, lists, slots = prepare(
        cand_owner.reshape(REQ, 1), cand_local.reshape(REQ, 1), held, companies
    )
    qall, slab, mine = spread(qt, cat, lists)
    part = pool(mine, qall, cat, slab)
    return finish(part, slots)


def solution(mesh):
    placed = (
        P("art", "seq", None, None),
        P(("art", "seq"), None, None),
        P(("art", "seq"), None, None),
        P("art", None, None),
    )
    return jax.shard_map(
        per_device,
        mesh=mesh,
        in_specs=placed,
        out_specs=(P(("art", "seq"), None), P(("art", "seq"), None)),
        check_vma=False,
    )
```

```python
import math

import jax
import jax.numpy as jnp
from jax import lax
from jax.experimental import pallas as pl
from jax.experimental.pallas import tpu as pltpu
from jax.sharding import PartitionSpec as P

EPS = 1e-06
SHARP = 16.0
TEMPER = 4.0
MESH = pl.DeviceIdType.MESH
HBM = pl.BlockSpec(memory_space=pl.ANY)
VMEM = pl.BlockSpec(memory_space=pltpu.VMEM)

NX, NY, NZ = 4, 4, 8
ARTS = 12
PART = ARTS // NX
LQ, LC, E = 256, 64, 128
NC = 64
C_DEV = 256
CAP = 18
GROUP = 6
GROUPS = CAP // GROUP
WORKERS = NZ * 2
REQ = ARTS * NC
SPLIT = 160
QUARTER = SPLIT // NX
HALF = QUARTER // 2
REST = (C_DEV - SPLIT) // 2


def unit(values):
    wide = values.astype(jnp.float32)
    return wide * lax.rsqrt(jnp.sum(wide * wide, axis=-1, keepdims=True) + EPS)


def place():
    art, x = lax.axis_index("art"), lax.axis_index("seq")
    return art // (NY * 2), (art // 2) % NY, art % 2, x


def prepare_kernel(own_ref, loc_ref, q_ref, c_ref, qt_ref, cat_ref, list_ref, slot_ref):
    def normalise(i, carry):
        cat_ref[pl.ds(i * 8, 8)] = unit(c_ref[pl.ds(i * 8, 8)]).astype(jnp.bfloat16)
        return carry

    lax.fori_loop(0, c_ref.shape[0] // 8, normalise, 0)
    for a in range(PART):
        qt_ref[a] = jnp.transpose(unit(q_ref[a])).astype(jnp.bfloat16)

    @pl.when(pl.program_id(0) == 0)
    def _():
        z, y, c, x = place()
        owner = own_ref[...]
        local = loc_ref[...]
        oz, oy, oc = owner // (NY * 2), (owner // 2) % NY, owner % 2
        lane = lax.broadcasted_iota(jnp.int32, (REQ, 128), 1)
        row = lax.broadcasted_iota(jnp.int32, (REQ, 1), 0)
        hot = lane == (oz * 2 + oc) * NY + oy
        table = jnp.where(hot, 1.0, 0.0).astype(jnp.bfloat16)
        first = lax.broadcasted_iota(jnp.int32, (REQ, REQ), 0)
        second = lax.broadcasted_iota(jnp.int32, (REQ, REQ), 1)
        before = jnp.where(second < first, 1.0, 0.0).astype(jnp.bfloat16)
        counts = jnp.dot(before, table, preferred_element_type=jnp.float32)
        rank = jnp.sum(jnp.where(hot, counts, 0.0), axis=1, keepdims=True).astype(jnp.int32)
        article = row // NC
        held = article % NX
        spot = ((x - held + NX) % NX) * PART + article // NX
        value = jnp.where(lane < 64, spot, local)
        entry = jnp.where(lane % 64 == rank, value, 0).astype(jnp.float32).astype(jnp.bfloat16)
        lists = lax.dot_general(
            table, entry, (((0,), (0,)), ((), ())), preferred_element_type=jnp.float32
        )
        lists = lists[: WORKERS * NY].astype(jnp.int32)
        for w in range(WORKERS):
            list_ref[w, 0:NY] = lists[w * NY : (w + 1) * NY]
            list_ref[w, NY:8] = jnp.zeros((8 - NY, 128), jnp.int32)
        side = ((z - oz + NZ) % NZ) * 2 + jnp.where(oc == c, 0, 1)
        column = ((oy - y + NY) % NY) * GROUPS + rank // GROUP
        slot_ref[...] = jnp.where(lane < 64, side * 8 + rank % GROUP, column)


def prepare(owners, locals_, queries, companies):
    steps = NX
    blocks = C_DEV // steps
    return pl.pallas_call(
        prepare_kernel,
        grid=(steps,),
        out_shape=(
            jax.ShapeDtypeStruct((ARTS, E, LQ), jnp.bfloat16),
            jax.ShapeDtypeStruct((C_DEV, LC, E), jnp.bfloat16),
            jax.ShapeDtypeStruct((WORKERS, 8, 128), jnp.int32),
            jax.ShapeDtypeStruct((REQ, 128), jnp.int32),
        ),
        in_specs=[
            pl.BlockSpec((REQ, 1), lambda i: (0, 0)),
            pl.BlockSpec((REQ, 1), lambda i: (0, 0)),
            pl.BlockSpec((PART, LQ, E), lambda i: (i, 0, 0)),
            pl.BlockSpec((blocks, LC, E), lambda i: (i, 0, 0)),
        ],
        out_specs=(
            pl.BlockSpec((PART, E, LQ), lambda i: (i, 0, 0)),
            pl.BlockSpec((blocks, LC, E), lambda i: (i, 0, 0)),
            pl.BlockSpec((WORKERS, 8, 128), lambda i: (0, 0, 0)),
            pl.BlockSpec((REQ, 128), lambda i: (0, 0)),
        ),
    )(owners, locals_, queries, companies)


N_COPIES = 100


def meet_kernel(
    qt_ref, cat_ref, list_ref, back_ref,
    qall_ref, cat0, cat1, cat2, cat3, lrecv_ref, lists, part_ref, send_sem, recv_sem, local_sem,
):
    slabs = (cat1, cat2, cat3)
    z, y, c, x = place()

    def at(dz=0, dy=0, dc=0, dx=0):
        zz, yy, cc, xx = (z + dz + NZ) % NZ, (y + dy + NY) % NY, (c + dc) % 2, (x + dx + NX) % NX
        return ((zz * NY + yy) * 2 + cc, xx)

    peers = [at(dz=-d, dc=k) for d in range(NZ) for k in range(2) if d or k]
    peers += [at(dy=1), at(dy=-1), at(dx=1), at(dx=2), at(dx=3)]
    barrier = pltpu.get_barrier_semaphore()
    for peer in peers:
        pl.semaphore_signal(barrier, inc=1, device_id=peer, device_id_type=MESH)
    pl.semaphore_wait(barrier, len(peers))

    copies = {}

    def send(name, src, dst, device):
        assert name not in copies
        n = len(copies)
        copy = pltpu.make_async_remote_copy(
            src_ref=src,
            dst_ref=dst,
            send_sem=send_sem.at[n],
            recv_sem=recv_sem.at[n],
            device_id=device,
            device_id_type=MESH,
        )
        copies[name] = copy
        copy.start()

    received = set()

    def got(*names):
        for name in names:
            if name not in received:
                received.add(name)
                copies[name].wait_recv()

    own_list = pltpu.make_async_copy(list_ref.at[z * 2 + c], lrecv_ref.at[0], local_sem.at[0])
    own_list.start()
    for d in range(NZ):
        for k in range(2):
            if d or k:
                worker = ((z - d + NZ) % NZ) * 2 + (c + k) % 2
                send(f"l{d}{k}", list_ref.at[worker], lrecv_ref.at[d * 2 + k], at(dz=-d, dc=k))

    own_cat = pltpu.make_async_copy(cat_ref, cat0, local_sem.at[2])
    own_cat.start()
    lane = lax.broadcasted_iota(jnp.int32, (8, 128), 1)

    own_part = pltpu.make_async_copy(
        qt_ref.at[pl.ds(x * PART, PART)], qall_ref.at[0, 0, pl.ds(0, PART)], local_sem.at[1]
    )
    own_part.start()
    for j in (1, 3, 2):
        send(
            f"e{j}",
            qt_ref.at[pl.ds(((x + j) % NX) * PART, PART)],
            qall_ref.at[0, 0, pl.ds(j * PART, PART)],
            at(dx=j),
        )

    def z_first(j):
        rows = pl.ds(j * PART, PART)
        src = qt_ref.at[pl.ds(x * PART, PART)] if j == 0 else qall_ref.at[0, 0, rows]
        send(f"p1{j}", src, qall_ref.at[NZ - 1, 0, rows], at(dz=1))
        send(f"m1{j}", src, qall_ref.at[1, 0, rows], at(dz=-1))

    def z_next(step, half, both=(True, True)):
        rows = pl.ds(half * 2 * PART, 2 * PART)
        if both[0]:
            send(f"p{step}{half}", qall_ref.at[NZ - step + 1, 0, rows], qall_ref.at[NZ - step, 0, rows], at(dz=1))
        if both[1]:
            send(f"m{step}{half}", qall_ref.at[step - 1, 0, rows], qall_ref.at[step, 0, rows], at(dz=-1))

    def partner(dz):
        send(f"c{dz}", qall_ref.at[dz, 0], qall_ref.at[dz, 1], at(dc=1))

    def quarter(of, h):
        return pl.ds(((x + of + NX) % NX) * QUARTER + h * HALF, HALF)

    def rest(h):
        return pl.ds(SPLIT + h * REST, REST)

    def y_own(tag, rows, h):
        def up():
            send(f"up{tag}{h}", cat_ref.at[rows(h)], slabs[2].at[rows(h)], at(dy=1))

        def down():
            send(f"dn{tag}{h}", cat_ref.at[rows(h)], slabs[0].at[rows(h)], at(dy=-1))

        return up, down

    def y_fwd(tag, rows):
        send(f"up2{tag}", slabs[2].at[rows(0)], slabs[1].at[rows(0)], at(dy=1))
        send(f"dn2{tag}", slabs[0].at[rows(1)], slabs[1].at[rows(1)], at(dy=-1))

    def x_own(d, h):
        rows = quarter(0, h)
        send(f"xp{d}{h}", slabs[d].at[rows], slabs[d].at[rows], at(dx=1))
        send(f"xm{d}{h}", slabs[d].at[rows], slabs[d].at[rows], at(dx=-1))

    def x_fwd(d):
        got(f"xp{d}0")
        rows = quarter(-1, 0)
        send(f"xpf{d}", slabs[d].at[rows], slabs[d].at[rows], at(dx=1))
        got(f"xm{d}1")
        rows = quarter(1, 1)
        send(f"xmf{d}", slabs[d].at[rows], slabs[d].at[rows], at(dx=-1))

    mine = lambda h: quarter(0, h)
    y_own("s", mine, 0)[0]()
    y_own("s", mine, 1)[1]()
    y_own("s", mine, 1)[0]()
    y_own("s", mine, 0)[1]()
    z_first(0)
    got("e1")
    z_first(1)
    got("e3")
    z_first(3)
    got("ups0", "dns1")
    y_fwd("s", mine)
    for h in (0, 1):
        y_own("r", rest, h)[0]()
        y_own("r", rest, 1 - h)[1]()
    x_own(2, 0)
    x_own(0, 1)
    got("e2")
    z_first(2)
    own_list.wait()
    got(*[n for n in copies if n[0] == "l"])
    list_copy = pltpu.make_async_copy(lrecv_ref, lists, local_sem.at[3])
    list_copy.start()
    own_part.wait()
    partner(0)
    got("p10", "p11", "m10", "m11")
    z_next(2, 0)
    got("ups1", "dns0")
    x_own(2, 1)
    x_own(0, 0)
    got("p12", "p13", "m12", "m13")
    z_next(2, 1)
    partner(NZ - 1)
    partner(1)
    got("up2s", "dn2s")
    x_own(1, 0)
    x_own(1, 1)
    got("p20", "m20")
    z_next(3, 0)
    x_fwd(2)
    x_fwd(0)
    got("p21", "m21")
    z_next(3, 1)
    partner(NZ - 2)
    partner(2)
    got("upr0", "dnr1")
    y_fwd("r", rest)
    got("p30")
    z_next(4, 0, (True, False))
    got("m30", "m31")
    z_next(4, 1, (False, True))
    got("p31")
    partner(NZ - 3)
    partner(3)
    x_fwd(1)
    got("p40", "m41")
    partner(4)
    got(*[n for n in copies if n[0] in "epmc"])

    def score(d):
        cat = (cat0, cat1, cat2, cat3)[d]
        owner = (y + d) % NY

        def tile(dz, carry):
            for k in range(2):
                w = dz * 2 + k
                scores = jnp.zeros((8, 128), jnp.float32) if d == 0 else part_ref[w]
                for g in range(GROUPS):
                    rows = []
                    for u in range(GROUP):
                        slot = g * GROUP + u
                        query = qall_ref[dz, k, lists[w, owner, slot]]
                        block = cat[lists[w, owner, 64 + slot]]
                        sims = jnp.dot(block, query, preferred_element_type=jnp.float32)
                        mass = jnp.exp2(sims * (SHARP * math.log2(math.e)))
                        rows.append(jnp.sum(jnp.sum(mass.reshape(8, 8, LQ), axis=0), axis=0, keepdims=True))
                    rows += [jnp.ones((8 - GROUP, LQ), jnp.float32)]
                    logs = jnp.log(jnp.concatenate(rows, axis=0))
                    total = jnp.sum(logs, axis=1, keepdims=True) * (1.0 / SHARP)
                    scores = jnp.where(lane == d * GROUPS + g, total, scores)
                part_ref[w] = scores
            return carry

        lax.fori_loop(0, NZ, tile, 0)

    own_cat.wait()
    list_copy.wait()
    score(0)
    got("dns0", "dns1", "dnr0", "dnr1", "xp00", "xp01", "xm00", "xm01", "xpf0", "xmf0")
    score(1)
    got("ups0", "ups1", "upr0", "upr1", "xp20", "xp21", "xm20", "xm21", "xpf2", "xmf2")
    score(3)
    for name in list(copies):
        got(name)
    score(2)
    own_part = pltpu.make_async_copy(part_ref.at[0], back_ref.at[0], local_sem.at[0])
    own_part.start()
    for d in range(NZ):
        for k in range(2):
            if d or k:
                send(f"b{d}{k}", part_ref.at[d * 2 + k], back_ref.at[d * 2 + k], at(dz=d, dc=k))
    own_part.wait()
    for name in list(copies):
        got(name)
    for copy in copies.values():
        copy.wait_send()


def meet(qt, cat, lists):
    return pl.pallas_call(
        meet_kernel,
        out_shape=jax.ShapeDtypeStruct((WORKERS, 8, 128), jnp.float32),
        in_specs=[HBM, HBM, HBM],
        out_specs=VMEM,
        scratch_shapes=[pltpu.VMEM((NZ, 2, ARTS, E, LQ), jnp.bfloat16)]
        + [pltpu.VMEM((C_DEV, LC, E), jnp.bfloat16)] * NY
        + [
            pltpu.VMEM((WORKERS, 8, 128), jnp.int32),
            pltpu.SMEM((WORKERS, 8, 128), jnp.int32),
            pltpu.VMEM((WORKERS, 8, 128), jnp.float32),
            pltpu.SemaphoreType.DMA((N_COPIES,)),
            pltpu.SemaphoreType.DMA((N_COPIES,)),
            pltpu.SemaphoreType.DMA((4,)),
        ],
        compiler_params=pltpu.CompilerParams(
            collective_id=0, has_side_effects=True, vmem_limit_bytes=48 << 20
        ),
    )(qt, cat, lists)


def finish_kernel(recv_ref, slot_ref, rel_ref, prob_ref):
    lane = lax.broadcasted_iota(jnp.int32, (REQ, 128), 1)
    slots = slot_ref[...]
    hot_row = jnp.where(lane == slots[:, 0:1], 1.0, 0.0).astype(jnp.bfloat16)
    hot_lane = lane == slots[:, 64:65]
    values = recv_ref[...].reshape(128, 128)
    picked = jnp.zeros((REQ, 128), jnp.float32)
    for _ in range(3):
        head = values.astype(jnp.bfloat16)
        picked = picked + jnp.dot(hot_row, head, preferred_element_type=jnp.float32)
        values = values - head.astype(jnp.float32)
    score = jnp.sum(jnp.where(hot_lane, picked, 0.0), axis=1, keepdims=True)
    wide = lax.broadcasted_iota(jnp.int32, (NC, 128), 1)
    columns = jnp.zeros((NC, 128), jnp.float32)
    for a in range(ARTS):
        columns = jnp.where(wide == a, score[a * NC : (a + 1) * NC], columns)
    relevance = columns - jnp.sum(columns, axis=0, keepdims=True) * (1.0 / NC)
    weights = jnp.exp(TEMPER * relevance)
    probs = weights / jnp.sum(weights, axis=0, keepdims=True)
    both = jnp.transpose(jnp.concatenate([relevance, probs], axis=0))
    rel_ref[...] = both[0:ARTS, 0:NC]
    prob_ref[...] = both[0:ARTS, NC:]


def finish(part, slots):
    return pl.pallas_call(
        finish_kernel,
        out_shape=(jax.ShapeDtypeStruct((ARTS, NC), jnp.float32),) * 2,
        in_specs=[VMEM, VMEM],
        out_specs=(VMEM, VMEM),
    )(part, slots)


def per_device(queries, cand_owner, cand_local, companies):
    held = queries.reshape(ARTS, LQ, E)
    qt, cat, lists, slots = prepare(
        cand_owner.reshape(REQ, 1), cand_local.reshape(REQ, 1), held, companies
    )
    return finish(meet(qt, cat, lists), slots)


def solution(mesh):
    placed = (
        P("art", "seq", None, None),
        P(("art", "seq"), None, None),
        P(("art", "seq"), None, None),
        P("art", None, None),
    )
    return jax.shard_map(
        per_device,
        mesh=mesh,
        in_specs=placed,
        out_specs=(P(("art", "seq"), None), P(("art", "seq"), None)),
        check_vma=False,
    )
```

```python
import math

import jax
import jax.numpy as jnp
from jax import lax
from jax.experimental import pallas as pl
from jax.experimental.pallas import tpu as pltpu
from jax.sharding import PartitionSpec as P

EPS = 1e-06
SHARP = 16.0
TEMPER = 4.0
MESH = pl.DeviceIdType.MESH
HBM = pl.BlockSpec(memory_space=pl.ANY)
VMEM = pl.BlockSpec(memory_space=pltpu.VMEM)

NX, NY, NZ = 4, 4, 8
ARTS = 12
PART = ARTS // NX
LQ, LC, E = 256, 64, 128
NC = 64
ROWS, PER = 16, 4
C_DEV = 256
CAP = 18
GROUP = 6
GROUPS = CAP // GROUP
WORKERS = NZ * 2
REQ = ARTS * NC
SPLIT = 160
QUARTER = SPLIT // NX
HALF = QUARTER // 2
REST = (C_DEV - SPLIT) // 2
RING = (0, 7, 1, 6, 2, 5, 3, 4)
SPOT = {dz: i for i, dz in enumerate(RING)}
NEAR = 5
N_COPIES = 112


def unit(values):
    wide = values.astype(jnp.float32)
    return wide * lax.rsqrt(jnp.sum(wide * wide, axis=-1, keepdims=True) + EPS)


def place():
    art, x = lax.axis_index("art"), lax.axis_index("seq")
    return art // (NY * 2), (art // 2) % NY, art % 2, x


def column(ref):
    table = ref[...].reshape(ARTS * PER, ROWS)
    return jnp.concatenate([table[:, r : r + 1] for r in range(ROWS)], axis=0)


def list_kernel(own_ref, loc_ref, list_ref, slot_ref):
    z, y, c, x = place()
    owner, local = column(own_ref), column(loc_ref)
    oz, oy, oc = owner // (NY * 2), (owner // 2) % NY, owner % 2
    lane = lax.broadcasted_iota(jnp.int32, (REQ, 128), 1)
    row = lax.broadcasted_iota(jnp.int32, (REQ, 1), 0)
    hot = lane == (oz * 2 + oc) * NY + oy
    table = jnp.where(hot, 1.0, 0.0).astype(jnp.bfloat16)
    first = lax.broadcasted_iota(jnp.int32, (REQ, REQ), 0)
    second = lax.broadcasted_iota(jnp.int32, (REQ, REQ), 1)
    before = jnp.where(second < first, 1.0, 0.0).astype(jnp.bfloat16)
    counts = jnp.dot(before, table, preferred_element_type=jnp.float32)
    rank = jnp.sum(jnp.where(hot, counts, 0.0), axis=1, keepdims=True).astype(jnp.int32)
    article = (row % (ARTS * PER)) // PER
    spot = ((x - article % NX + NX) % NX) * PART + article // NX
    value = jnp.where(lane < 64, spot, local)
    entry = jnp.where(lane % 64 == rank, value, 0).astype(jnp.float32).astype(jnp.bfloat16)
    lists = lax.dot_general(table, entry, (((0,), (0,)), ((), ())), preferred_element_type=jnp.float32)
    lists = lists[: WORKERS * NY].astype(jnp.int32)
    for w in range(WORKERS):
        list_ref[w, 0:NY] = lists[w * NY : (w + 1) * NY]
        list_ref[w, NY:8] = jnp.zeros((8 - NY, 128), jnp.int32)
    dz = (z - oz + NZ) % NZ
    ring = jnp.where(dz < NZ // 2, 2 * dz, 2 * (NZ - dz) - 1)
    side = ring * 2 + jnp.where(oc == c, 0, 1)
    spot_lane = ((oy - y + NY) % NY) * GROUPS + rank // GROUP
    slot_ref[...] = jnp.where(lane < 64, side * 8 + rank % GROUP, spot_lane)


def make_lists(owners, locals_):
    return pl.pallas_call(
        list_kernel,
        out_shape=(
            jax.ShapeDtypeStruct((WORKERS, 8, 128), jnp.int32),
            jax.ShapeDtypeStruct((REQ, 128), jnp.int32),
        ),
        in_specs=[VMEM, VMEM],
        out_specs=(VMEM, VMEM),
    )(owners, locals_)


def meet_kernel(
    list_ref, q_hbm, c_hbm, back_ref,
    raw_ref, qt_ref, near_ref, far_ref, cat0, cat1, cat2, cat3,
    lrecv_ref, lists, part_ref, send_sem, recv_sem, local_sem,
):
    slabs = (cat1, cat2, cat3)
    z, y, c, x = place()

    def at(dz=0, dy=0, dc=0, dx=0):
        zz, yy, cc, xx = (z + dz + NZ) % NZ, (y + dy + NY) % NY, (c + dc) % 2, (x + dx + NX) % NX
        return ((zz * NY + yy) * 2 + cc, xx)

    peers = [at(dz=-d, dc=k) for d in range(NZ) for k in range(2) if d or k]
    peers += [at(dy=1), at(dy=-1), at(dx=1), at(dx=2), at(dx=3)]
    barrier = pltpu.get_barrier_semaphore()
    for peer in peers:
        pl.semaphore_signal(barrier, inc=1, device_id=peer, device_id_type=MESH)

    def load(src, dst, n):
        copy = pltpu.make_async_copy(src, dst, local_sem.at[n])
        copy.start()
        return copy

    def quarter(of, h):
        return pl.ds(((x + of + NX) % NX) * QUARTER + h * HALF, HALF)

    def rest(h):
        return pl.ds(SPLIT + h * REST, REST)

    whole = [pl.ds(((x + of) % NX) * QUARTER, QUARTER) for of in range(NX)]
    tail = pl.ds(SPLIT, C_DEV - SPLIT)
    in_first = load(c_hbm.at[whole[0]], cat0.at[whole[0]], 0)
    in_query = load(q_hbm, raw_ref, 1)
    in_tail = load(c_hbm.at[tail], cat0.at[tail], 2)
    in_other = [load(c_hbm.at[whole[of]], cat0.at[whole[of]], 2 + of) for of in (1, 2, 3)]

    def normalise(start, count):
        def some(i, carry):
            rows = pl.ds(start + i * 8, 8)
            cat0[rows] = unit(cat0[rows]).astype(jnp.bfloat16)
            return carry

        lax.fori_loop(0, count // 8, some, 0)

    in_first.wait()
    normalise(x * QUARTER, QUARTER)
    in_query.wait()
    for a in range(ARTS):
        qt_ref[a] = jnp.transpose(unit(raw_ref[a])).astype(jnp.bfloat16)
    for m in range(PART):
        near_ref[0, 0, m] = qt_ref[x * PART + m]
    pl.semaphore_wait(barrier, len(peers))

    copies = {}

    def send(name, src, dst, device):
        assert name not in copies
        n = len(copies)
        copy = pltpu.make_async_remote_copy(
            src_ref=src,
            dst_ref=dst,
            send_sem=send_sem.at[n],
            recv_sem=recv_sem.at[n],
            device_id=device,
            device_id_type=MESH,
        )
        copies[name] = copy
        copy.start()

    received = set()

    def got(*names):
        for name in names:
            if name not in received:
                received.add(name)
                copies[name].wait_recv()

    def tile(dz, k):
        i = SPOT[dz]
        return near_ref.at[i, k] if i < NEAR else far_ref.at[i - NEAR, k]

    def z_first(j):
        rows = pl.ds(j * PART, PART)
        src = tile(0, 0).at[rows]
        send(f"p1{j}", src, tile(NZ - 1, 0).at[rows], at(dz=1))
        send(f"m1{j}", src, tile(1, 0).at[rows], at(dz=-1))

    def z_next(step, half, both=(True, True)):
        rows = pl.ds(half * 2 * PART, 2 * PART)
        if both[0]:
            send(f"p{step}{half}", tile(NZ - step + 1, 0).at[rows], tile(NZ - step, 0).at[rows], at(dz=1))
        if both[1]:
            send(f"m{step}{half}", tile(step - 1, 0).at[rows], tile(step, 0).at[rows], at(dz=-1))

    def partner(dz):
        send(f"c{dz}", tile(dz, 0), tile(dz, 1), at(dc=1))

    def y_up(tag, rows, h):
        send(f"up{tag}{h}", cat0.at[rows(h)], slabs[2].at[rows(h)], at(dy=1))

    def y_down(tag, rows, h):
        send(f"dn{tag}{h}", cat0.at[rows(h)], slabs[0].at[rows(h)], at(dy=-1))

    def y_fwd(tag, rows):
        send(f"upf{tag}", slabs[2].at[rows(0)], slabs[1].at[rows(0)], at(dy=1))
        send(f"dnf{tag}", slabs[0].at[rows(1)], slabs[1].at[rows(1)], at(dy=-1))

    def x_own(d, h):
        rows = quarter(0, h)
        send(f"xp{d}{h}", slabs[d].at[rows], slabs[d].at[rows], at(dx=1))
        send(f"xm{d}{h}", slabs[d].at[rows], slabs[d].at[rows], at(dx=-1))

    def x_fwd(d):
        got(f"xp{d}0")
        rows = quarter(-1, 0)
        send(f"xpf{d}", slabs[d].at[rows], slabs[d].at[rows], at(dx=1))
        got(f"xm{d}1")
        rows = quarter(1, 1)
        send(f"xmf{d}", slabs[d].at[rows], slabs[d].at[rows], at(dx=-1))

    def mine(h):
        return quarter(0, h)

    y_up("s", mine, 0)
    y_down("s", mine, 1)
    y_up("s", mine, 1)
    y_down("s", mine, 0)
    for j in (1, 3, 2):
        send(
            f"e{j}",
            qt_ref.at[pl.ds(((x + j) % NX) * PART, PART)],
            tile(0, 0).at[pl.ds(j * PART, PART)],
            at(dx=j),
        )
    z_first(0)
    in_tail.wait()
    normalise(SPLIT, C_DEV - SPLIT)
    got("e1")
    z_first(1)
    got("e3")
    z_first(3)
    got("ups0", "dns1")
    y_fwd("s", mine)
    for h in (0, 1):
        y_up("r", rest, h)
        y_down("r", rest, 1 - h)
    x_own(2, 0)
    x_own(0, 1)
    got("e2")
    z_first(2)
    partner(0)
    got("p10", "p11", "m10", "m11")
    z_next(2, 0)
    own_list = load(list_ref.at[z * 2 + c], lrecv_ref.at[0], 0)
    for d in range(NZ):
        for k in range(2):
            if d or k:
                worker = ((z - d + NZ) % NZ) * 2 + (c + k) % 2
                send(f"l{d}{k}", list_ref.at[worker], lrecv_ref.at[SPOT[d] * 2 + k], at(dz=-d, dc=k))
    got("ups1", "dns0")
    x_own(2, 1)
    x_own(0, 0)
    got("p12", "p13", "m12", "m13")
    z_next(2, 1)
    partner(NZ - 1)
    partner(1)
    got("upfs", "dnfs")
    x_own(1, 0)
    x_own(1, 1)
    own_list.wait()
    got(*[n for n in copies if n[0] == "l"])
    lists_in = load(lrecv_ref, lists, 0)
    for of in (1, 2, 3):
        in_other[of - 1].wait()
        normalise(((x + of) % NX) * QUARTER, QUARTER)
    got("p20", "m20")
    z_next(3, 0)
    x_fwd(2)
    x_fwd(0)
    got("p21", "m21")
    z_next(3, 1)
    partner(NZ - 2)
    partner(2)
    got("upr0", "dnr1")
    y_fwd("r", rest)
    lists_in.wait()

    lane = lax.broadcasted_iota(jnp.int32, (8, 128), 1)
    cats = (cat0, cat1, cat2, cat3)

    def score(d, queries, i, base):
        owner = (y + d) % NY
        for k in range(2):
            w = (base + i) * 2 + k
            scores = jnp.zeros((8, 128), jnp.float32) if d == 0 else part_ref[w]
            for g in range(GROUPS):
                rows = []
                for u in range(GROUP):
                    slot = g * GROUP + u
                    query = queries[i, k, lists[w, owner, slot]]
                    block = cats[d][lists[w, owner, 64 + slot]]
                    sims = jnp.dot(block, query, preferred_element_type=jnp.float32)
                    mass = jnp.exp2(sims * (SHARP * math.log2(math.e)))
                    rows.append(jnp.sum(jnp.sum(mass.reshape(8, 8, LQ), axis=0), axis=0, keepdims=True))
                rows += [jnp.ones((8 - GROUP, LQ), jnp.float32)]
                logs = jnp.log(jnp.concatenate(rows, axis=0))
                total = jnp.sum(logs, axis=1, keepdims=True) * (1.0 / SHARP)
                scores = jnp.where(lane == d * GROUPS + g, total, scores)
            part_ref[w] = scores

    def wave(d, far):
        queries, base, count = (far_ref, NEAR, NZ - NEAR) if far else (near_ref, 0, NEAR)

        def body(i, carry):
            score(d, queries, i, base)
            return carry

        lax.fori_loop(0, count, body, 0)

    got("c0", "c1", f"c{NZ - 1}", "c2", f"c{NZ - 2}")
    wave(0, False)
    got("p30")
    z_next(4, 0, (True, False))
    x_fwd(1)
    got("m30", "m31")
    z_next(4, 1, (False, True))
    got("p31")
    partner(NZ - 3)
    partner(3)
    got("dns0", "dns1", "dnr0", "dnr1", "xp00", "xp01", "xm00", "xm01", "xpf0", "xmf0")
    wave(1, False)
    got("p40", "m41")
    partner(4)
    got("ups0", "ups1", "upr0", "upr1", "xp20", "xp21", "xm20", "xm21", "xpf2", "xmf2")
    wave(3, False)
    got(*[n for n in copies if n[0] == "c"])
    wave(0, True)
    wave(1, True)
    wave(3, True)
    for name in list(copies):
        got(name)

    def back(i):
        for k in range(2):
            d, n = RING[i], i * 2 + k
            if d or k:
                send(f"b{d}{k}", part_ref.at[n], back_ref.at[n], at(dz=d, dc=k))

    wave(2, True)
    for i in range(NZ - 1, NEAR - 1, -1):
        back(i)
    wave(2, False)
    for i in range(NEAR - 1, -1, -1):
        back(i)
    own_part = load(part_ref.at[0], back_ref.at[0], 0)
    own_part.wait()
    for name in list(copies):
        got(name)
    for copy in copies.values():
        copy.wait_send()


def meet(lists, queries, companies):
    return pl.pallas_call(
        meet_kernel,
        out_shape=jax.ShapeDtypeStruct((WORKERS, 8, 128), jnp.float32),
        in_specs=[HBM, HBM, HBM],
        out_specs=VMEM,
        scratch_shapes=[
            pltpu.VMEM((ARTS, LQ, E), jnp.bfloat16),
            pltpu.VMEM((ARTS, E, LQ), jnp.bfloat16),
            pltpu.VMEM((NEAR, 2, ARTS, E, LQ), jnp.bfloat16),
            pltpu.VMEM((NZ - NEAR, 2, ARTS, E, LQ), jnp.bfloat16),
        ]
        + [pltpu.VMEM((C_DEV, LC, E), jnp.bfloat16)] * NY
        + [
            pltpu.VMEM((WORKERS, 8, 128), jnp.int32),
            pltpu.SMEM((WORKERS, 8, 128), jnp.int32),
            pltpu.VMEM((WORKERS, 8, 128), jnp.float32),
            pltpu.SemaphoreType.DMA((N_COPIES,)),
            pltpu.SemaphoreType.DMA((N_COPIES,)),
            pltpu.SemaphoreType.DMA((6,)),
        ],
        compiler_params=pltpu.CompilerParams(
            collective_id=0, has_side_effects=True, vmem_limit_bytes=60 << 20
        ),
    )(lists, queries, companies)


def gather_rows(hot, values, dims):
    total = None
    for _ in range(3):
        head = values.astype(jnp.bfloat16)
        term = lax.dot_general(hot, head, (dims, ((), ())), preferred_element_type=jnp.float32)
        total = term if total is None else total + term
        values = values - head.astype(jnp.float32)
    return total


def finish_kernel(recv_ref, slot_ref, rel_ref, prob_ref):
    lane = lax.broadcasted_iota(jnp.int32, (REQ, 128), 1)
    row = lax.broadcasted_iota(jnp.int32, (REQ, 1), 0)
    slots = slot_ref[...]
    hot_row = jnp.where(lane == slots[:, 0:1], 1.0, 0.0).astype(jnp.bfloat16)
    picked = gather_rows(hot_row, recv_ref[...].reshape(128, 128), ((1,), (0,)))
    score = jnp.sum(jnp.where(lane == slots[:, 64:65], picked, 0.0), axis=1, keepdims=True)
    step = row % (ARTS * PER)
    hot_article = jnp.where(lane == step // PER, 1.0, 0.0).astype(jnp.bfloat16)
    candidate = (row // (ARTS * PER)) * PER + step % PER
    placed = jnp.where(lane == candidate, score, 0.0)
    table = gather_rows(hot_article, placed, ((0,), (0,)))[0:16, 0:NC]
    relevance = table - jnp.sum(table, axis=1, keepdims=True) * (1.0 / NC)
    weights = jnp.exp(TEMPER * relevance)
    probs = weights / jnp.sum(weights, axis=1, keepdims=True)
    rel_ref[...] = relevance[0:ARTS]
    prob_ref[...] = probs[0:ARTS]


def finish(part, slots):
    return pl.pallas_call(
        finish_kernel,
        out_shape=(jax.ShapeDtypeStruct((ARTS, NC), jnp.float32),) * 2,
        in_specs=[VMEM, VMEM],
        out_specs=(VMEM, VMEM),
    )(part, slots)


def per_device(queries, cand_owner, cand_local, companies):
    held = queries.reshape(ARTS, LQ, E)
    owners = jnp.transpose(cand_owner, (0, 2, 1))
    locals_ = jnp.transpose(cand_local, (0, 2, 1))
    lists, slots = make_lists(owners, locals_)
    return finish(meet(lists, held, companies), slots)


def solution(mesh):
    placed = (
        P("art", "seq", None, None),
        P(("art", "seq"), None, None),
        P(("art", "seq"), None, None),
        P("art", None, None),
    )
    return jax.shard_map(
        per_device,
        mesh=mesh,
        in_specs=placed,
        out_specs=(P(("art", "seq"), None), P(("art", "seq"), None)),
        check_vma=False,
    )
```

```python
import math

import jax
import jax.numpy as jnp
from jax import lax
from jax.experimental import pallas as pl
from jax.experimental.pallas import tpu as pltpu
from jax.sharding import PartitionSpec as P

EPS = 1e-06
SHARP = 16.0
TEMPER = 4.0
MESH = pl.DeviceIdType.MESH
HBM = pl.BlockSpec(memory_space=pl.ANY)
VMEM = pl.BlockSpec(memory_space=pltpu.VMEM)

NX, NY, NZ = 4, 4, 8
ARTS = 12
PART = ARTS // NX
LQ, LC, E = 256, 64, 128
NC = 64
ROWS, PER = 16, 4
C_DEV = 256
CAP = 18
GROUP = 6
GROUPS = CAP // GROUP
WORKERS = NZ * 2
REQ = ARTS * NC
SPLIT = 160
QUARTER = SPLIT // NX
HALF = QUARTER // 2
REST = (C_DEV - SPLIT) // 2
RING = (0, 7, 1, 6, 2, 5, 3, 4)
SPOT = {dz: i for i, dz in enumerate(RING)}
NEAR = 5
N_COPIES = 112


def unit(values):
    wide = values.astype(jnp.float32)
    return wide * lax.rsqrt(jnp.sum(wide * wide, axis=-1, keepdims=True) + EPS)


def place():
    art, x = lax.axis_index("art"), lax.axis_index("seq")
    return art // (NY * 2), (art // 2) % NY, art % 2, x


def column(ref):
    table = ref[...].reshape(ARTS * PER, ROWS)
    return jnp.concatenate([table[:, r : r + 1] for r in range(ROWS)], axis=0)


def list_kernel(own_ref, loc_ref, list_ref, slot_ref):
    z, y, c, x = place()
    owner, local = column(own_ref), column(loc_ref)
    oz, oy, oc = owner // (NY * 2), (owner // 2) % NY, owner % 2
    lane = lax.broadcasted_iota(jnp.int32, (REQ, 128), 1)
    row = lax.broadcasted_iota(jnp.int32, (REQ, 1), 0)
    hot = lane == (oz * 2 + oc) * NY + oy
    table = jnp.where(hot, 1.0, 0.0).astype(jnp.bfloat16)
    first = lax.broadcasted_iota(jnp.int32, (REQ, REQ), 0)
    second = lax.broadcasted_iota(jnp.int32, (REQ, REQ), 1)
    before = jnp.where(second < first, 1.0, 0.0).astype(jnp.bfloat16)
    counts = jnp.dot(before, table, preferred_element_type=jnp.float32)
    rank = jnp.sum(jnp.where(hot, counts, 0.0), axis=1, keepdims=True).astype(jnp.int32)
    article = (row % (ARTS * PER)) // PER
    spot = ((x - article % NX + NX) % NX) * PART + article // NX
    value = jnp.where(lane < 64, spot, local)
    entry = jnp.where(lane % 64 == rank, value, 0).astype(jnp.float32).astype(jnp.bfloat16)
    lists = lax.dot_general(table, entry, (((0,), (0,)), ((), ())), preferred_element_type=jnp.float32)
    lists = lists[: WORKERS * NY].astype(jnp.int32)
    for w in range(WORKERS):
        list_ref[w, 0:NY] = lists[w * NY : (w + 1) * NY]
        list_ref[w, NY:8] = jnp.zeros((8 - NY, 128), jnp.int32)
    dz = (z - oz + NZ) % NZ
    ring = jnp.where(dz < NZ // 2, 2 * dz, 2 * (NZ - dz) - 1)
    side = ring * 2 + jnp.where(oc == c, 0, 1)
    spot_lane = ((oy - y + NY) % NY) * GROUPS + rank // GROUP
    slot_ref[...] = jnp.where(lane < 64, side * 8 + rank % GROUP, spot_lane)


def make_lists(owners, locals_):
    return pl.pallas_call(
        list_kernel,
        out_shape=(
            jax.ShapeDtypeStruct((WORKERS, 8, 128), jnp.int32),
            jax.ShapeDtypeStruct((REQ, 128), jnp.int32),
        ),
        in_specs=[VMEM, VMEM],
        out_specs=(VMEM, VMEM),
    )(owners, locals_)


def meet_kernel(
    list_ref, q_hbm, c_hbm, back_ref,
    raw_ref, qt_ref, near_ref, far_ref, cat0, cat1, cat2, cat3,
    lrecv_ref, lists, part_ref, send_sem, recv_sem, local_sem,
):
    slabs = (cat1, cat2, cat3)
    z, y, c, x = place()

    def at(dz=0, dy=0, dc=0, dx=0):
        zz, yy, cc, xx = (z + dz + NZ) % NZ, (y + dy + NY) % NY, (c + dc) % 2, (x + dx + NX) % NX
        return ((zz * NY + yy) * 2 + cc, xx)

    peers = [at(dz=-d, dc=k) for d in range(NZ) for k in range(2) if d or k]
    peers += [at(dy=1), at(dy=-1), at(dx=1), at(dx=2), at(dx=3)]
    barrier = pltpu.get_barrier_semaphore()
    for peer in peers:
        pl.semaphore_signal(barrier, inc=1, device_id=peer, device_id_type=MESH)

    def load(src, dst, n):
        copy = pltpu.make_async_copy(src, dst, local_sem.at[n])
        copy.start()
        return copy

    def quarter(of, h):
        return pl.ds(((x + of + NX) % NX) * QUARTER + h * HALF, HALF)

    def rest(h):
        return pl.ds(SPLIT + h * REST, REST)

    whole = [pl.ds(((x + of) % NX) * QUARTER, QUARTER) for of in range(NX)]
    tail = pl.ds(SPLIT, C_DEV - SPLIT)
    in_first = load(c_hbm.at[whole[0]], cat0.at[whole[0]], 0)
    in_query = load(q_hbm, raw_ref, 1)
    in_tail = load(c_hbm.at[tail], cat0.at[tail], 2)
    in_other = [load(c_hbm.at[whole[of]], cat0.at[whole[of]], 2 + of) for of in (1, 2, 3)]

    def normalise(start, count):
        def some(i, carry):
            rows = pl.ds(start + i * 8, 8)
            cat0[rows] = unit(cat0[rows]).astype(jnp.bfloat16)
            return carry

        lax.fori_loop(0, count // 8, some, 0)

    in_first.wait()
    normalise(x * QUARTER, QUARTER)
    in_query.wait()
    for a in range(ARTS):
        qt_ref[a] = jnp.transpose(unit(raw_ref[a])).astype(jnp.bfloat16)
    for m in range(PART):
        near_ref[0, 0, m] = qt_ref[x * PART + m]
    pl.semaphore_wait(barrier, len(peers))

    copies = {}

    def send(name, src, dst, device):
        assert name not in copies
        n = len(copies)
        copy = pltpu.make_async_remote_copy(
            src_ref=src,
            dst_ref=dst,
            send_sem=send_sem.at[n],
            recv_sem=recv_sem.at[n],
            device_id=device,
            device_id_type=MESH,
        )
        copies[name] = copy
        copy.start()

    received = set()

    def got(*names):
        for name in names:
            if name not in received:
                received.add(name)
                copies[name].wait_recv()

    def tile(dz, k):
        i = SPOT[dz]
        return near_ref.at[i, k] if i < NEAR else far_ref.at[i - NEAR, k]

    def z_first(j):
        rows = pl.ds(j * PART, PART)
        src = tile(0, 0).at[rows]
        send(f"p1{j}", src, tile(NZ - 1, 0).at[rows], at(dz=1))
        send(f"m1{j}", src, tile(1, 0).at[rows], at(dz=-1))

    def z_next(step, half, both=(True, True)):
        rows = pl.ds(half * 2 * PART, 2 * PART)
        if both[0]:
            send(f"p{step}{half}", tile(NZ - step + 1, 0).at[rows], tile(NZ - step, 0).at[rows], at(dz=1))
        if both[1]:
            send(f"m{step}{half}", tile(step - 1, 0).at[rows], tile(step, 0).at[rows], at(dz=-1))

    def partner(dz):
        send(f"c{dz}", tile(dz, 0), tile(dz, 1), at(dc=1))

    def y_up(tag, rows, h):
        send(f"up{tag}{h}", cat0.at[rows(h)], slabs[2].at[rows(h)], at(dy=1))

    def y_down(tag, rows, h):
        send(f"dn{tag}{h}", cat0.at[rows(h)], slabs[0].at[rows(h)], at(dy=-1))

    def y_fwd(tag, rows):
        send(f"upf{tag}", slabs[2].at[rows(0)], slabs[1].at[rows(0)], at(dy=1))
        send(f"dnf{tag}", slabs[0].at[rows(1)], slabs[1].at[rows(1)], at(dy=-1))

    def x_own(d, h):
        rows = quarter(0, h)
        send(f"xp{d}{h}", slabs[d].at[rows], slabs[d].at[rows], at(dx=1))
        send(f"xm{d}{h}", slabs[d].at[rows], slabs[d].at[rows], at(dx=-1))

    def x_fwd(d):
        got(f"xp{d}0")
        rows = quarter(-1, 0)
        send(f"xpf{d}", slabs[d].at[rows], slabs[d].at[rows], at(dx=1))
        got(f"xm{d}1")
        rows = quarter(1, 1)
        send(f"xmf{d}", slabs[d].at[rows], slabs[d].at[rows], at(dx=-1))

    def mine(h):
        return quarter(0, h)

    y_up("s", mine, 0)
    y_down("s", mine, 1)
    y_up("s", mine, 1)
    y_down("s", mine, 0)
    for j in (1, 3, 2):
        send(
            f"e{j}",
            qt_ref.at[pl.ds(((x + j) % NX) * PART, PART)],
            tile(0, 0).at[pl.ds(j * PART, PART)],
            at(dx=j),
        )
    z_first(0)
    in_tail.wait()
    normalise(SPLIT, C_DEV - SPLIT)
    got("e1")
    z_first(1)
    got("e3")
    z_first(3)
    got("ups0", "dns1")
    y_fwd("s", mine)
    for h in (0, 1):
        y_up("r", rest, h)
        y_down("r", rest, 1 - h)
    x_own(2, 0)
    x_own(0, 1)
    got("e2")
    z_first(2)
    partner(0)
    got("p10", "p11", "m10", "m11")
    z_next(2, 0)
    own_list = load(list_ref.at[z * 2 + c], lrecv_ref.at[0], 0)
    for d in range(NZ):
        for k in range(2):
            if d or k:
                worker = ((z - d + NZ) % NZ) * 2 + (c + k) % 2
                send(f"l{d}{k}", list_ref.at[worker], lrecv_ref.at[SPOT[d] * 2 + k], at(dz=-d, dc=k))
    got("ups1", "dns0")
    x_own(2, 1)
    x_own(0, 0)
    got("p12", "p13", "m12", "m13")
    z_next(2, 1)
    partner(NZ - 1)
    partner(1)
    got("upfs", "dnfs")
    x_own(1, 0)
    x_own(1, 1)
    own_list.wait()
    got(*[n for n in copies if n[0] == "l"])
    lists_in = load(lrecv_ref, lists, 0)
    for of in (1, 2, 3):
        in_other[of - 1].wait()
        normalise(((x + of) % NX) * QUARTER, QUARTER)
    got("p20", "m20")
    z_next(3, 0)
    x_fwd(2)
    x_fwd(0)
    got("p21", "m21")
    z_next(3, 1)
    partner(NZ - 2)
    partner(2)
    got("upr0", "dnr1")
    y_fwd("r", rest)
    lists_in.wait()

    lane = lax.broadcasted_iota(jnp.int32, (8, 128), 1)
    cats = (cat0, cat1, cat2, cat3)

    def score(d, queries, i, base):
        owner = (y + d) % NY
        for k in range(2):
            w = (base + i) * 2 + k
            scores = jnp.zeros((8, 128), jnp.float32) if d == 0 else part_ref[w]
            for g in range(GROUPS):
                rows = []
                for u in range(GROUP):
                    slot = g * GROUP + u
                    query = queries[i, k, lists[w, owner, slot]]
                    block = cats[d][lists[w, owner, 64 + slot]]
                    sims = jnp.dot(block, query, preferred_element_type=jnp.float32)
                    mass = jnp.exp2(sims * (SHARP * math.log2(math.e)))
                    rows.append(jnp.sum(jnp.sum(mass.reshape(8, 8, LQ), axis=0), axis=0, keepdims=True))
                rows += [jnp.ones((8 - GROUP, LQ), jnp.float32)]
                logs = jnp.log(jnp.concatenate(rows, axis=0))
                total = jnp.sum(logs, axis=1, keepdims=True) * (1.0 / SHARP)
                scores = jnp.where(lane == d * GROUPS + g, total, scores)
            part_ref[w] = scores

    def wave(d, far):
        queries, base, count = (far_ref, NEAR, NZ - NEAR) if far else (near_ref, 0, NEAR)

        def body(i, carry):
            score(d, queries, i, base)
            return carry

        lax.fori_loop(0, count, body, 0, unroll=(d == 2))

    got("c0", "c1", f"c{NZ - 1}", "c2", f"c{NZ - 2}")
    wave(0, False)
    got("p30")
    z_next(4, 0, (True, False))
    x_fwd(1)
    got("m30", "m31")
    z_next(4, 1, (False, True))
    got("p31")
    partner(NZ - 3)
    partner(3)
    got("ups0", "ups1", "upr0", "upr1", "xp20", "xp21", "xm20", "xm21", "xpf2", "xmf2")
    wave(3, False)
    got("p40", "m41")
    partner(4)
    got(*[n for n in copies if n[0] == "c"])
    wave(0, True)
    wave(3, True)
    got("dns0", "dns1", "dnr0", "dnr1", "xp00", "xp01", "xm00", "xm01", "xpf0", "xmf0")
    wave(1, False)
    wave(1, True)
    for name in list(copies):
        got(name)

    def back(i):
        for k in range(2):
            d, n = RING[i], i * 2 + k
            if d or k:
                send(f"b{d}{k}", part_ref.at[n], back_ref.at[n], at(dz=d, dc=k))

    wave(2, True)
    for i in range(NZ - 1, NEAR - 1, -1):
        back(i)
    wave(2, False)
    for i in range(NEAR - 1, -1, -1):
        back(i)
    own_part = load(part_ref.at[0], back_ref.at[0], 0)
    own_part.wait()
    for name in list(copies):
        got(name)
    for copy in copies.values():
        copy.wait_send()


def meet(lists, queries, companies):
    return pl.pallas_call(
        meet_kernel,
        out_shape=jax.ShapeDtypeStruct((WORKERS, 8, 128), jnp.float32),
        in_specs=[HBM, HBM, HBM],
        out_specs=VMEM,
        scratch_shapes=[
            pltpu.VMEM((ARTS, LQ, E), jnp.bfloat16),
            pltpu.VMEM((ARTS, E, LQ), jnp.bfloat16),
            pltpu.VMEM((NEAR, 2, ARTS, E, LQ), jnp.bfloat16),
            pltpu.VMEM((NZ - NEAR, 2, ARTS, E, LQ), jnp.bfloat16),
        ]
        + [pltpu.VMEM((C_DEV, LC, E), jnp.bfloat16)] * NY
        + [
            pltpu.VMEM((WORKERS, 8, 128), jnp.int32),
            pltpu.SMEM((WORKERS, 8, 128), jnp.int32),
            pltpu.VMEM((WORKERS, 8, 128), jnp.float32),
            pltpu.SemaphoreType.DMA((N_COPIES,)),
            pltpu.SemaphoreType.DMA((N_COPIES,)),
            pltpu.SemaphoreType.DMA((6,)),
        ],
        compiler_params=pltpu.CompilerParams(
            collective_id=0, has_side_effects=True, vmem_limit_bytes=60 << 20
        ),
    )(lists, queries, companies)


def gather_rows(hot, values, dims):
    total = None
    for _ in range(3):
        head = values.astype(jnp.bfloat16)
        term = lax.dot_general(hot, head, (dims, ((), ())), preferred_element_type=jnp.float32)
        total = term if total is None else total + term
        values = values - head.astype(jnp.float32)
    return total


def finish_kernel(recv_ref, slot_ref, rel_ref, prob_ref):
    lane = lax.broadcasted_iota(jnp.int32, (REQ, 128), 1)
    row = lax.broadcasted_iota(jnp.int32, (REQ, 1), 0)
    slots = slot_ref[...]
    hot_row = jnp.where(lane == slots[:, 0:1], 1.0, 0.0).astype(jnp.bfloat16)
    picked = gather_rows(hot_row, recv_ref[...].reshape(128, 128), ((1,), (0,)))
    score = jnp.sum(jnp.where(lane == slots[:, 64:65], picked, 0.0), axis=1, keepdims=True)
    step = row % (ARTS * PER)
    hot_article = jnp.where(lane == step // PER, 1.0, 0.0).astype(jnp.bfloat16)
    candidate = (row // (ARTS * PER)) * PER + step % PER
    placed = jnp.where(lane == candidate, score, 0.0)
    table = gather_rows(hot_article, placed, ((0,), (0,)))[0:16, 0:NC]
    relevance = table - jnp.sum(table, axis=1, keepdims=True) * (1.0 / NC)
    weights = jnp.exp(TEMPER * relevance)
    probs = weights / jnp.sum(weights, axis=1, keepdims=True)
    rel_ref[...] = relevance[0:ARTS]
    prob_ref[...] = probs[0:ARTS]


def finish(part, slots):
    return pl.pallas_call(
        finish_kernel,
        out_shape=(jax.ShapeDtypeStruct((ARTS, NC), jnp.float32),) * 2,
        in_specs=[VMEM, VMEM],
        out_specs=(VMEM, VMEM),
    )(part, slots)


def per_device(queries, cand_owner, cand_local, companies):
    held = queries.reshape(ARTS, LQ, E)
    owners = jnp.transpose(cand_owner, (0, 2, 1))
    locals_ = jnp.transpose(cand_local, (0, 2, 1))
    lists, slots = make_lists(owners, locals_)
    return finish(meet(lists, held, companies), slots)


def solution(mesh):
    placed = (
        P("art", "seq", None, None),
        P(("art", "seq"), None, None),
        P(("art", "seq"), None, None),
        P("art", None, None),
    )
    return jax.shard_map(
        per_device,
        mesh=mesh,
        in_specs=placed,
        out_specs=(P(("art", "seq"), None), P(("art", "seq"), None)),
        check_vma=False,
    )
```

```python
import math

import jax
import jax.numpy as jnp
from jax import lax
from jax.experimental import pallas as pl
from jax.experimental.pallas import tpu as pltpu
from jax.sharding import PartitionSpec as P

EPS = 1e-06
SHARP = 16.0
TEMPER = 4.0
MESH = pl.DeviceIdType.MESH
HBM = pl.BlockSpec(memory_space=pl.ANY)
VMEM = pl.BlockSpec(memory_space=pltpu.VMEM)

NX, NY, NZ = 4, 4, 8
ARTS = 12
PART = ARTS // NX
LQ, LC, E = 256, 64, 128
NC = 64
ROWS, PER = 16, 4
C_DEV = 256
CAP = 18
GROUP = 6
GROUPS = CAP // GROUP
WORKERS = NZ * 2
REQ = ARTS * NC
SPLIT = 160
QUARTER = SPLIT // NX
HALF = QUARTER // 2
REST = (C_DEV - SPLIT) // 2
RING = (0, 7, 1, 6, 2, 5, 3, 4)
SPOT = {dz: i for i, dz in enumerate(RING)}
NEAR = 5
N_COPIES = 112


def unit(values):
    wide = values.astype(jnp.float32)
    return wide * lax.rsqrt(jnp.sum(wide * wide, axis=-1, keepdims=True) + EPS)


def place():
    art, x = lax.axis_index("art"), lax.axis_index("seq")
    return art // (NY * 2), (art // 2) % NY, art % 2, x


def list_kernel(own_ref, loc_ref, list_ref, slot_ref):
    z, y, c, x = place()
    owner = own_ref[...].reshape(ARTS * PER, ROWS)
    local = loc_ref[...].reshape(ARTS * PER, ROWS)
    oz, oy, oc = owner >> 3, (owner >> 1) & 3, owner & 1
    dz = (z - oz) & (NZ - 1)
    ring = jnp.where(dz < NZ // 2, 2 * dz, 2 * (NZ - dz) - 1)
    side = ring * 2 + ((oc + c) & 1)
    packed = (((side * 4 + ((oy - y) & 3)) * 64 + (oz * 2 + oc) * NY + oy) * 256) + local
    packed = jnp.concatenate([packed[:, r : r + 1] for r in range(ROWS)], axis=0)
    lane = lax.broadcasted_iota(jnp.int32, (REQ, 128), 1)
    wide = jnp.broadcast_to(packed, (REQ, 128))
    hot = lane == ((wide >> 8) & 63)
    marks = jnp.where(hot, 1.0, 0.0)
    table = marks.astype(jnp.bfloat16)
    first = lax.broadcasted_iota(jnp.int32, (128, 128), 0)
    second = lax.broadcasted_iota(jnp.int32, (128, 128), 1)
    before = jnp.where(second < first, 1.0, 0.0).astype(jnp.bfloat16)
    seen = jnp.zeros((1, 128), jnp.float32)
    ranks = []
    for i in range(REQ // 128):
        some = slice(i * 128, (i + 1) * 128)
        counts = jnp.dot(before, table[some], preferred_element_type=jnp.float32) + seen
        ranks.append(jnp.sum(jnp.where(hot[some], counts, 0.0), axis=1, keepdims=True))
        seen = seen + jnp.sum(marks[some], axis=0, keepdims=True)
    rank = jnp.broadcast_to(jnp.concatenate(ranks, axis=0).astype(jnp.int32), (REQ, 128))
    step = lax.broadcasted_iota(jnp.int32, (ARTS * PER, 128), 0)
    article = step >> 2
    spot = ((x - article) & 3) * PART + (article >> 2)
    spot = jnp.concatenate([spot] * ROWS, axis=0)
    value = jnp.where(lane < 64, spot, wide & 255)
    entry = jnp.where((lane & 63) == rank, value, 0).astype(jnp.float32).astype(jnp.bfloat16)
    lists = lax.dot_general(table, entry, (((0,), (0,)), ((), ())), preferred_element_type=jnp.float32)
    lists = lists[: WORKERS * NY].astype(jnp.int32)
    for w in range(WORKERS):
        list_ref[w, 0:NY] = lists[w * NY : (w + 1) * NY]
        list_ref[w, NY:8] = jnp.zeros((8 - NY, 128), jnp.int32)
    line = (rank * 43) >> 8
    slot_ref[...] = jnp.where(
        lane < 64, (wide >> 16) * 8 + rank - line * GROUP, ((wide >> 14) & 3) * GROUPS + line
    )


def make_lists(owners, locals_):
    return pl.pallas_call(
        list_kernel,
        out_shape=(
            jax.ShapeDtypeStruct((WORKERS, 8, 128), jnp.int32),
            jax.ShapeDtypeStruct((REQ, 128), jnp.int32),
        ),
        in_specs=[VMEM, VMEM],
        out_specs=(VMEM, VMEM),
    )(owners, locals_)


def meet_kernel(
    list_ref, q_hbm, c_hbm, back_ref,
    raw_ref, qt_ref, near_ref, far_ref, cat0, cat1, cat2, cat3,
    lrecv_ref, lists, part_ref, send_sem, recv_sem, local_sem,
):
    slabs = (cat1, cat2, cat3)
    z, y, c, x = place()

    def at(dz=0, dy=0, dc=0, dx=0):
        zz, yy, cc, xx = (z + dz + NZ) % NZ, (y + dy + NY) % NY, (c + dc) % 2, (x + dx + NX) % NX
        return ((zz * NY + yy) * 2 + cc, xx)

    peers = [at(dz=-d, dc=k) for d in range(NZ) for k in range(2) if d or k]
    peers += [at(dy=1), at(dy=-1), at(dx=1), at(dx=2), at(dx=3)]
    barrier = pltpu.get_barrier_semaphore()
    for peer in peers:
        pl.semaphore_signal(barrier, inc=1, device_id=peer, device_id_type=MESH)

    def load(src, dst, n):
        copy = pltpu.make_async_copy(src, dst, local_sem.at[n])
        copy.start()
        return copy

    def quarter(of, h):
        return pl.ds(((x + of + NX) % NX) * QUARTER + h * HALF, HALF)

    def rest(h):
        return pl.ds(SPLIT + h * REST, REST)

    whole = [pl.ds(((x + of) % NX) * QUARTER, QUARTER) for of in range(NX)]
    tail = pl.ds(SPLIT, C_DEV - SPLIT)
    in_first = load(c_hbm.at[whole[0]], cat0.at[whole[0]], 0)
    in_query = load(q_hbm, raw_ref, 1)
    in_tail = load(c_hbm.at[tail], cat0.at[tail], 2)
    in_other = [load(c_hbm.at[whole[of]], cat0.at[whole[of]], 2 + of) for of in (1, 2, 3)]

    def normalise(start, count):
        def some(i, carry):
            rows = pl.ds(start + i * 8, 8)
            cat0[rows] = unit(cat0[rows]).astype(jnp.bfloat16)
            return carry

        lax.fori_loop(0, count // 8, some, 0)

    in_first.wait()
    normalise(x * QUARTER, QUARTER)
    in_query.wait()
    for a in range(ARTS):
        qt_ref[a] = jnp.transpose(unit(raw_ref[a])).astype(jnp.bfloat16)
    for m in range(PART):
        near_ref[0, 0, m] = qt_ref[x * PART + m]
    pl.semaphore_wait(barrier, len(peers))

    copies = {}

    def send(name, src, dst, device):
        assert name not in copies
        n = len(copies)
        copy = pltpu.make_async_remote_copy(
            src_ref=src,
            dst_ref=dst,
            send_sem=send_sem.at[n],
            recv_sem=recv_sem.at[n],
            device_id=device,
            device_id_type=MESH,
        )
        copies[name] = copy
        copy.start()

    received = set()

    def got(*names):
        for name in names:
            if name not in received:
                received.add(name)
                copies[name].wait_recv()

    def tile(dz, k):
        i = SPOT[dz]
        return near_ref.at[i, k] if i < NEAR else far_ref.at[i - NEAR, k]

    def z_first(j):
        rows = pl.ds(j * PART, PART)
        src = tile(0, 0).at[rows]
        send(f"p1{j}", src, tile(NZ - 1, 0).at[rows], at(dz=1))
        send(f"m1{j}", src, tile(1, 0).at[rows], at(dz=-1))

    def z_next(step, half, both=(True, True)):
        rows = pl.ds(half * 2 * PART, 2 * PART)
        if both[0]:
            send(f"p{step}{half}", tile(NZ - step + 1, 0).at[rows], tile(NZ - step, 0).at[rows], at(dz=1))
        if both[1]:
            send(f"m{step}{half}", tile(step - 1, 0).at[rows], tile(step, 0).at[rows], at(dz=-1))

    def partner(dz):
        send(f"c{dz}", tile(dz, 0), tile(dz, 1), at(dc=1))

    def y_up(tag, rows, h):
        send(f"up{tag}{h}", cat0.at[rows(h)], slabs[2].at[rows(h)], at(dy=1))

    def y_down(tag, rows, h):
        send(f"dn{tag}{h}", cat0.at[rows(h)], slabs[0].at[rows(h)], at(dy=-1))

    def y_fwd(tag, rows):
        send(f"upf{tag}", slabs[2].at[rows(0)], slabs[1].at[rows(0)], at(dy=1))
        send(f"dnf{tag}", slabs[0].at[rows(1)], slabs[1].at[rows(1)], at(dy=-1))

    def x_own(d, h):
        rows = quarter(0, h)
        send(f"xp{d}{h}", slabs[d].at[rows], slabs[d].at[rows], at(dx=1))
        send(f"xm{d}{h}", slabs[d].at[rows], slabs[d].at[rows], at(dx=-1))

    def x_fwd(d):
        got(f"xp{d}0")
        rows = quarter(-1, 0)
        send(f"xpf{d}", slabs[d].at[rows], slabs[d].at[rows], at(dx=1))
        got(f"xm{d}1")
        rows = quarter(1, 1)
        send(f"xmf{d}", slabs[d].at[rows], slabs[d].at[rows], at(dx=-1))

    def mine(h):
        return quarter(0, h)

    y_up("s", mine, 0)
    y_down("s", mine, 1)
    y_up("s", mine, 1)
    y_down("s", mine, 0)
    for j in (1, 3, 2):
        send(
            f"e{j}",
            qt_ref.at[pl.ds(((x + j) % NX) * PART, PART)],
            tile(0, 0).at[pl.ds(j * PART, PART)],
            at(dx=j),
        )
    z_first(0)
    in_tail.wait()
    normalise(SPLIT, C_DEV - SPLIT)
    got("e1")
    z_first(1)
    got("e3")
    z_first(3)
    got("ups0", "dns1")
    y_fwd("s", mine)
    for h in (0, 1):
        y_up("r", rest, h)
        y_down("r", rest, 1 - h)
    x_own(2, 0)
    x_own(0, 1)
    got("e2")
    z_first(2)
    partner(0)
    got("p10", "p11", "m10", "m11")
    z_next(2, 0)
    own_list = load(list_ref.at[z * 2 + c], lrecv_ref.at[0], 0)
    for d in range(NZ):
        for k in range(2):
            if d or k:
                worker = ((z - d + NZ) % NZ) * 2 + (c + k) % 2
                send(f"l{d}{k}", list_ref.at[worker], lrecv_ref.at[SPOT[d] * 2 + k], at(dz=-d, dc=k))
    got("ups1", "dns0")
    x_own(2, 1)
    x_own(0, 0)
    got("p12", "p13", "m12", "m13")
    z_next(2, 1)
    partner(NZ - 1)
    partner(1)
    got("upfs", "dnfs")
    x_own(1, 0)
    x_own(1, 1)
    own_list.wait()
    got(*[n for n in copies if n[0] == "l"])
    lists_in = load(lrecv_ref, lists, 0)
    for of in (1, 2, 3):
        in_other[of - 1].wait()
        normalise(((x + of) % NX) * QUARTER, QUARTER)
    got("p20", "m20")
    z_next(3, 0)
    x_fwd(2)
    x_fwd(0)
    got("p21", "m21")
    z_next(3, 1)
    partner(NZ - 2)
    partner(2)
    got("upr0", "dnr1")
    y_fwd("r", rest)
    lists_in.wait()

    lane = lax.broadcasted_iota(jnp.int32, (8, 128), 1)
    cats = (cat0, cat1, cat2, cat3)

    def score(d, queries, i, base):
        owner = (y + d) % NY
        for k in range(2):
            w = (base + i) * 2 + k
            scores = jnp.zeros((8, 128), jnp.float32) if d == 0 else part_ref[w]
            for g in range(GROUPS):
                rows = []
                for u in range(GROUP):
                    slot = g * GROUP + u
                    query = queries[i, k, lists[w, owner, slot]]
                    block = cats[d][lists[w, owner, 64 + slot]]
                    sims = jnp.dot(block, query, preferred_element_type=jnp.float32)
                    mass = jnp.exp2(sims * (SHARP * math.log2(math.e)))
                    rows.append(jnp.sum(jnp.sum(mass.reshape(8, 8, LQ), axis=0), axis=0, keepdims=True))
                rows += [jnp.ones((8 - GROUP, LQ), jnp.float32)]
                logs = jnp.log(jnp.concatenate(rows, axis=0))
                total = jnp.sum(logs, axis=1, keepdims=True) * (1.0 / SHARP)
                scores = jnp.where(lane == d * GROUPS + g, total, scores)
            part_ref[w] = scores

    def wave(d, far):
        queries, base, count = (far_ref, NEAR, NZ - NEAR) if far else (near_ref, 0, NEAR)

        def body(i, carry):
            score(d, queries, i, base)
            return carry

        lax.fori_loop(0, count, body, 0, unroll=(d == 2))

    got("c0", "c1", f"c{NZ - 1}", "c2", f"c{NZ - 2}")
    wave(0, False)
    got("p30")
    z_next(4, 0, (True, False))
    x_fwd(1)
    got("m30", "m31")
    z_next(4, 1, (False, True))
    got("p31")
    partner(NZ - 3)
    partner(3)
    got("ups0", "ups1", "upr0", "upr1", "xp20", "xp21", "xm20", "xm21", "xpf2", "xmf2")
    wave(3, False)
    got("p40", "m41")
    partner(4)
    got(*[n for n in copies if n[0] == "c"])
    wave(0, True)
    wave(3, True)
    got("dns0", "dns1", "dnr0", "dnr1", "xp00", "xp01", "xm00", "xm01", "xpf0", "xmf0")
    wave(1, False)
    wave(1, True)
    for name in list(copies):
        got(name)

    def back(i):
        for k in range(2):
            d, n = RING[i], i * 2 + k
            if d or k:
                send(f"b{d}{k}", part_ref.at[n], back_ref.at[n], at(dz=d, dc=k))

    wave(2, True)
    for i in range(NZ - 1, NEAR - 1, -1):
        back(i)
    wave(2, False)
    for i in range(NEAR - 1, -1, -1):
        back(i)
    own_part = load(part_ref.at[0], back_ref.at[0], 0)
    own_part.wait()
    for name in list(copies):
        got(name)
    for copy in copies.values():
        copy.wait_send()


def meet(lists, queries, companies):
    return pl.pallas_call(
        meet_kernel,
        out_shape=jax.ShapeDtypeStruct((WORKERS, 8, 128), jnp.float32),
        in_specs=[HBM, HBM, HBM],
        out_specs=VMEM,
        scratch_shapes=[
            pltpu.VMEM((ARTS, LQ, E), jnp.bfloat16),
            pltpu.VMEM((ARTS, E, LQ), jnp.bfloat16),
            pltpu.VMEM((NEAR, 2, ARTS, E, LQ), jnp.bfloat16),
            pltpu.VMEM((NZ - NEAR, 2, ARTS, E, LQ), jnp.bfloat16),
        ]
        + [pltpu.VMEM((C_DEV, LC, E), jnp.bfloat16)] * NY
        + [
            pltpu.VMEM((WORKERS, 8, 128), jnp.int32),
            pltpu.SMEM((WORKERS, 8, 128), jnp.int32),
            pltpu.VMEM((WORKERS, 8, 128), jnp.float32),
            pltpu.SemaphoreType.DMA((N_COPIES,)),
            pltpu.SemaphoreType.DMA((N_COPIES,)),
            pltpu.SemaphoreType.DMA((6,)),
        ],
        compiler_params=pltpu.CompilerParams(
            collective_id=0, has_side_effects=True, vmem_limit_bytes=60 << 20
        ),
    )(lists, queries, companies)


def gather_rows(hot, values):
    total = None
    for _ in range(3):
        head = values.astype(jnp.bfloat16)
        term = jnp.dot(hot, head, preferred_element_type=jnp.float32)
        total = term if total is None else total + term
        values = values - head.astype(jnp.float32)
    return total


def finish_kernel(recv_ref, slot_ref, rel_ref, prob_ref):
    lane = lax.broadcasted_iota(jnp.int32, (REQ, 128), 1)
    slots = slot_ref[...]
    hot_row = jnp.where(lane == slots[:, 0:1], 1.0, 0.0).astype(jnp.bfloat16)
    picked = gather_rows(hot_row, recv_ref[...].reshape(128, 128))
    score = jnp.sum(jnp.where(lane == slots[:, 64:65], picked, 0.0), axis=1, keepdims=True)
    step = lax.broadcasted_iota(jnp.int32, (ARTS * PER, 128), 0)
    wide = lax.broadcasted_iota(jnp.int32, (ARTS * PER, 128), 1)
    table = jnp.zeros((ARTS * PER, 128), jnp.float32)
    for r in range(ROWS):
        mine = score[r * ARTS * PER : (r + 1) * ARTS * PER]
        table = jnp.where(wide == r * PER + (step & 3), mine, table)
    table = jnp.sum(table.reshape(ARTS, PER, 128), axis=1)[:, 0:NC]
    relevance = table - jnp.sum(table, axis=1, keepdims=True) * (1.0 / NC)
    weights = jnp.exp(TEMPER * relevance)
    probs = weights / jnp.sum(weights, axis=1, keepdims=True)
    rel_ref[...] = relevance
    prob_ref[...] = probs


def finish(part, slots):
    return pl.pallas_call(
        finish_kernel,
        out_shape=(jax.ShapeDtypeStruct((ARTS, NC), jnp.float32),) * 2,
        in_specs=[VMEM, VMEM],
        out_specs=(VMEM, VMEM),
    )(part, slots)


def per_device(queries, cand_owner, cand_local, companies):
    held = queries.reshape(ARTS, LQ, E)
    owners = jnp.transpose(cand_owner, (0, 2, 1))
    locals_ = jnp.transpose(cand_local, (0, 2, 1))
    lists, slots = make_lists(owners, locals_)
    return finish(meet(lists, held, companies), slots)


def solution(mesh):
    placed = (
        P("art", "seq", None, None),
        P(("art", "seq"), None, None),
        P(("art", "seq"), None, None),
        P("art", None, None),
    )
    return jax.shard_map(
        per_device,
        mesh=mesh,
        in_specs=placed,
        out_specs=(P(("art", "seq"), None), P(("art", "seq"), None)),
        check_vma=False,
    )
```

```python
import math

import jax
import jax.numpy as jnp
from jax import lax
from jax.experimental import pallas as pl
from jax.experimental.pallas import tpu as pltpu
from jax.sharding import PartitionSpec as P

EPS = 1e-06
SHARP = 16.0
TEMPER = 4.0
MESH = pl.DeviceIdType.MESH
HBM = pl.BlockSpec(memory_space=pl.ANY)
VMEM = pl.BlockSpec(memory_space=pltpu.VMEM)

NX, NY, NZ = 4, 4, 8
ARTS = 12
PART = ARTS // NX
LQ, LC, E = 256, 64, 128
NC = 64
ROWS, PER = 16, 4
C_DEV = 256
CAP = 18
GROUP = 6
GROUPS = CAP // GROUP
WORKERS = NZ * 2
REQ = ARTS * NC
SPLIT = 160
QUARTER = SPLIT // NX
HALF = QUARTER // 2
REST = (C_DEV - SPLIT) // 2
RING = (0, 7, 1, 6, 2, 5, 3, 4)
SPOT = {dz: i for i, dz in enumerate(RING)}
NEAR = 5
N_COPIES = 112


def unit(values):
    wide = values.astype(jnp.float32)
    return wide * lax.rsqrt(jnp.sum(wide * wide, axis=-1, keepdims=True) + EPS)


def place():
    art, x = lax.axis_index("art"), lax.axis_index("seq")
    return art // (NY * 2), (art // 2) % NY, art % 2, x


def build(own_ref, loc_ref, list_ref, slot_ref):
    z, y, c, x = place()
    owner = own_ref[...].reshape(ARTS * PER, ROWS)
    local = loc_ref[...].reshape(ARTS * PER, ROWS)
    oz, oy, oc = owner >> 3, (owner >> 1) & 3, owner & 1
    dz = (z - oz) & (NZ - 1)
    ring = jnp.where(dz < NZ // 2, 2 * dz, 2 * (NZ - dz) - 1)
    side = ring * 2 + ((oc + c) & 1)
    packed = (((side * 4 + ((oy - y) & 3)) * 64 + (oz * 2 + oc) * NY + oy) * 256) + local
    packed = jnp.concatenate([packed[:, r : r + 1] for r in range(ROWS)], axis=0)
    lane = lax.broadcasted_iota(jnp.int32, (REQ, 128), 1)
    wide = jnp.broadcast_to(packed, (REQ, 128))
    hot = lane == ((wide >> 8) & 63)
    marks = jnp.where(hot, 1.0, 0.0)
    table = marks.astype(jnp.bfloat16)
    first = lax.broadcasted_iota(jnp.int32, (128, 128), 0)
    second = lax.broadcasted_iota(jnp.int32, (128, 128), 1)
    before = jnp.where(second < first, 1.0, 0.0).astype(jnp.bfloat16)
    seen = jnp.zeros((1, 128), jnp.float32)
    ranks = []
    for i in range(REQ // 128):
        some = slice(i * 128, (i + 1) * 128)
        counts = jnp.dot(before, table[some], preferred_element_type=jnp.float32) + seen
        ranks.append(jnp.sum(jnp.where(hot[some], counts, 0.0), axis=1, keepdims=True))
        seen = seen + jnp.sum(marks[some], axis=0, keepdims=True)
    rank = jnp.broadcast_to(jnp.concatenate(ranks, axis=0).astype(jnp.int32), (REQ, 128))
    step = lax.broadcasted_iota(jnp.int32, (ARTS * PER, 128), 0)
    article = step >> 2
    spot = ((x - article) & 3) * PART + (article >> 2)
    spot = jnp.concatenate([spot] * ROWS, axis=0)
    value = jnp.where(lane < 64, spot, wide & 255)
    entry = jnp.where((lane & 63) == rank, value, 0).astype(jnp.float32).astype(jnp.bfloat16)
    lists = lax.dot_general(table, entry, (((0,), (0,)), ((), ())), preferred_element_type=jnp.float32)
    lists = lists[: WORKERS * NY].astype(jnp.int32)
    for w in range(WORKERS):
        list_ref[w, 0:NY] = lists[w * NY : (w + 1) * NY]
        list_ref[w, NY:8] = jnp.zeros((8 - NY, 128), jnp.int32)
    line = (rank * 43) >> 8
    slot_ref[...] = jnp.where(
        lane < 64, (wide >> 16) * 8 + rank - line * GROUP, ((wide >> 14) & 3) * GROUPS + line
    )


def meet_kernel(
    own_ref, loc_ref, q_hbm, c_hbm, back_ref, slot_ref,
    raw_ref, qt_ref, near_ref, far_ref, cat0, cat1, cat2, cat3,
    list_ref, lrecv_ref, lists, part_ref, send_sem, recv_sem, local_sem,
):
    slabs = (cat1, cat2, cat3)
    z, y, c, x = place()

    def at(dz=0, dy=0, dc=0, dx=0):
        zz, yy, cc, xx = (z + dz + NZ) % NZ, (y + dy + NY) % NY, (c + dc) % 2, (x + dx + NX) % NX
        return ((zz * NY + yy) * 2 + cc, xx)

    peers = [at(dz=-d, dc=k) for d in range(NZ) for k in range(2) if d or k]
    peers += [at(dy=1), at(dy=-1), at(dx=1), at(dx=2), at(dx=3)]
    barrier = pltpu.get_barrier_semaphore()
    for peer in peers:
        pl.semaphore_signal(barrier, inc=1, device_id=peer, device_id_type=MESH)

    def load(src, dst, n):
        copy = pltpu.make_async_copy(src, dst, local_sem.at[n])
        copy.start()
        return copy

    def quarter(of, h):
        return pl.ds(((x + of + NX) % NX) * QUARTER + h * HALF, HALF)

    def rest(h):
        return pl.ds(SPLIT + h * REST, REST)

    whole = [pl.ds(((x + of) % NX) * QUARTER, QUARTER) for of in range(NX)]
    tail = pl.ds(SPLIT, C_DEV - SPLIT)
    in_first = load(c_hbm.at[whole[0]], cat0.at[whole[0]], 0)
    in_query = load(q_hbm, raw_ref, 1)
    in_tail = load(c_hbm.at[tail], cat0.at[tail], 2)
    in_other = [load(c_hbm.at[whole[of]], cat0.at[whole[of]], 2 + of) for of in (1, 2, 3)]

    def normalise(start, count):
        def some(i, carry):
            rows = pl.ds(start + i * 8, 8)
            cat0[rows] = unit(cat0[rows]).astype(jnp.bfloat16)
            return carry

        lax.fori_loop(0, count // 8, some, 0)

    in_first.wait()
    normalise(x * QUARTER, QUARTER)
    in_query.wait()
    for a in range(ARTS):
        qt_ref[a] = jnp.transpose(unit(raw_ref[a])).astype(jnp.bfloat16)
    for m in range(PART):
        near_ref[0, 0, m] = qt_ref[x * PART + m]
    pl.semaphore_wait(barrier, len(peers))

    copies = {}

    def send(name, src, dst, device):
        assert name not in copies
        n = len(copies)
        copy = pltpu.make_async_remote_copy(
            src_ref=src,
            dst_ref=dst,
            send_sem=send_sem.at[n],
            recv_sem=recv_sem.at[n],
            device_id=device,
            device_id_type=MESH,
        )
        copies[name] = copy
        copy.start()

    received = set()

    def got(*names):
        for name in names:
            if name not in received:
                received.add(name)
                copies[name].wait_recv()

    def tile(dz, k):
        i = SPOT[dz]
        return near_ref.at[i, k] if i < NEAR else far_ref.at[i - NEAR, k]

    def z_first(j):
        rows = pl.ds(j * PART, PART)
        src = tile(0, 0).at[rows]
        send(f"p1{j}", src, tile(NZ - 1, 0).at[rows], at(dz=1))
        send(f"m1{j}", src, tile(1, 0).at[rows], at(dz=-1))

    def z_next(step, half, both=(True, True)):
        rows = pl.ds(half * 2 * PART, 2 * PART)
        if both[0]:
            send(f"p{step}{half}", tile(NZ - step + 1, 0).at[rows], tile(NZ - step, 0).at[rows], at(dz=1))
        if both[1]:
            send(f"m{step}{half}", tile(step - 1, 0).at[rows], tile(step, 0).at[rows], at(dz=-1))

    def partner(dz):
        send(f"c{dz}", tile(dz, 0), tile(dz, 1), at(dc=1))

    def y_up(tag, rows, h):
        send(f"up{tag}{h}", cat0.at[rows(h)], slabs[2].at[rows(h)], at(dy=1))

    def y_down(tag, rows, h):
        send(f"dn{tag}{h}", cat0.at[rows(h)], slabs[0].at[rows(h)], at(dy=-1))

    def y_fwd(tag, rows):
        send(f"upf{tag}", slabs[2].at[rows(0)], slabs[1].at[rows(0)], at(dy=1))
        send(f"dnf{tag}", slabs[0].at[rows(1)], slabs[1].at[rows(1)], at(dy=-1))

    def x_own(d, h):
        rows = quarter(0, h)
        send(f"xp{d}{h}", slabs[d].at[rows], slabs[d].at[rows], at(dx=1))
        send(f"xm{d}{h}", slabs[d].at[rows], slabs[d].at[rows], at(dx=-1))

    def x_fwd(d):
        got(f"xp{d}0")
        rows = quarter(-1, 0)
        send(f"xpf{d}", slabs[d].at[rows], slabs[d].at[rows], at(dx=1))
        got(f"xm{d}1")
        rows = quarter(1, 1)
        send(f"xmf{d}", slabs[d].at[rows], slabs[d].at[rows], at(dx=-1))

    def mine(h):
        return quarter(0, h)

    y_up("s", mine, 0)
    y_down("s", mine, 1)
    y_up("s", mine, 1)
    y_down("s", mine, 0)
    for j in (1, 3, 2):
        send(
            f"e{j}",
            qt_ref.at[pl.ds(((x + j) % NX) * PART, PART)],
            tile(0, 0).at[pl.ds(j * PART, PART)],
            at(dx=j),
        )
    z_first(0)
    in_tail.wait()
    normalise(SPLIT, C_DEV - SPLIT)
    got("e1")
    z_first(1)
    got("e3")
    z_first(3)
    build(own_ref, loc_ref, list_ref, slot_ref)
    got("ups0", "dns1")
    y_fwd("s", mine)
    for h in (0, 1):
        y_up("r", rest, h)
        y_down("r", rest, 1 - h)
    x_own(2, 0)
    x_own(0, 1)
    got("e2")
    z_first(2)
    partner(0)
    got("p10", "p11", "m10", "m11")
    z_next(2, 0)
    own_list = load(list_ref.at[z * 2 + c], lrecv_ref.at[0], 0)
    for d in range(NZ):
        for k in range(2):
            if d or k:
                worker = ((z - d + NZ) % NZ) * 2 + (c + k) % 2
                send(f"l{d}{k}", list_ref.at[worker], lrecv_ref.at[SPOT[d] * 2 + k], at(dz=-d, dc=k))
    got("ups1", "dns0")
    x_own(2, 1)
    x_own(0, 0)
    got("p12", "p13", "m12", "m13")
    z_next(2, 1)
    partner(NZ - 1)
    partner(1)
    got("upfs", "dnfs")
    x_own(1, 0)
    x_own(1, 1)
    own_list.wait()
    got(*[n for n in copies if n[0] == "l"])
    lists_in = load(lrecv_ref, lists, 0)
    for of in (1, 2, 3):
        in_other[of - 1].wait()
        normalise(((x + of) % NX) * QUARTER, QUARTER)
    got("p20", "m20")
    z_next(3, 0)
    x_fwd(2)
    x_fwd(0)
    got("p21", "m21")
    z_next(3, 1)
    partner(NZ - 2)
    partner(2)
    got("upr0", "dnr1")
    y_fwd("r", rest)
    lists_in.wait()

    lane = lax.broadcasted_iota(jnp.int32, (8, 128), 1)
    cats = (cat0, cat1, cat2, cat3)

    def score(d, queries, i, base):
        owner = (y + d) % NY
        for k in range(2):
            w = (base + i) * 2 + k
            scores = jnp.zeros((8, 128), jnp.float32) if d == 0 else part_ref[w]
            for g in range(GROUPS):
                rows = []
                for u in range(GROUP):
                    slot = g * GROUP + u
                    query = queries[i, k, jnp.minimum(lists[w, owner, slot] & 15, ARTS - 1)]
                    block = cats[d][lists[w, owner, 64 + slot] & (C_DEV - 1)]
                    sims = jnp.dot(block, query, preferred_element_type=jnp.float32)
                    mass = jnp.exp2(sims * (SHARP * math.log2(math.e)))
                    rows.append(jnp.sum(jnp.sum(mass.reshape(8, 8, LQ), axis=0), axis=0, keepdims=True))
                rows += [jnp.ones((8 - GROUP, LQ), jnp.float32)]
                logs = jnp.log(jnp.concatenate(rows, axis=0))
                total = jnp.sum(logs, axis=1, keepdims=True) * (1.0 / SHARP)
                scores = jnp.where(lane == d * GROUPS + g, total, scores)
            part_ref[w] = scores

    def wave(d, far):
        queries, base, count = (far_ref, NEAR, NZ - NEAR) if far else (near_ref, 0, NEAR)

        def body(i, carry):
            score(d, queries, i, base)
            return carry

        lax.fori_loop(0, count, body, 0, unroll=(d == 2))

    got("c0", "c1", f"c{NZ - 1}", "c2", f"c{NZ - 2}")
    wave(0, False)
    got("p30")
    z_next(4, 0, (True, False))
    x_fwd(1)
    got("m30", "m31")
    z_next(4, 1, (False, True))
    got("p31")
    partner(NZ - 3)
    partner(3)
    got("ups0", "ups1", "upr0", "upr1", "xp20", "xp21", "xm20", "xm21", "xpf2", "xmf2")
    wave(3, False)
    got("p40", "m41")
    partner(4)
    got(*[n for n in copies if n[0] == "c"])
    wave(0, True)
    wave(3, True)
    got("dns0", "dns1", "dnr0", "dnr1", "xp00", "xp01", "xm00", "xm01", "xpf0", "xmf0")
    wave(1, False)
    wave(1, True)
    for name in list(copies):
        got(name)

    def back(i):
        for k in range(2):
            d, n = RING[i], i * 2 + k
            if d or k:
                send(f"b{d}{k}", part_ref.at[n], back_ref.at[n], at(dz=d, dc=k))

    wave(2, True)
    for i in range(NZ - 1, NEAR - 1, -1):
        back(i)
    wave(2, False)
    for i in range(NEAR - 1, -1, -1):
        back(i)
    own_part = load(part_ref.at[0], back_ref.at[0], 0)
    own_part.wait()
    for name in list(copies):
        got(name)
    for copy in copies.values():
        copy.wait_send()


def meet(owners, locals_, queries, companies):
    return pl.pallas_call(
        meet_kernel,
        out_shape=(
            jax.ShapeDtypeStruct((WORKERS, 8, 128), jnp.float32),
            jax.ShapeDtypeStruct((REQ, 128), jnp.int32),
        ),
        in_specs=[VMEM, VMEM, HBM, HBM],
        out_specs=(VMEM, VMEM),
        scratch_shapes=[
            pltpu.VMEM((ARTS, LQ, E), jnp.bfloat16),
            pltpu.VMEM((ARTS, E, LQ), jnp.bfloat16),
            pltpu.VMEM((NEAR, 2, ARTS, E, LQ), jnp.bfloat16),
            pltpu.VMEM((NZ - NEAR, 2, ARTS, E, LQ), jnp.bfloat16),
        ]
        + [pltpu.VMEM((C_DEV, LC, E), jnp.bfloat16)] * NY
        + [
            pltpu.VMEM((WORKERS, 8, 128), jnp.int32),
            pltpu.VMEM((WORKERS, 8, 128), jnp.int32),
            pltpu.SMEM((WORKERS, 8, 128), jnp.int32),
            pltpu.VMEM((WORKERS, 8, 128), jnp.float32),
            pltpu.SemaphoreType.DMA((N_COPIES,)),
            pltpu.SemaphoreType.DMA((N_COPIES,)),
            pltpu.SemaphoreType.DMA((6,)),
        ],
        compiler_params=pltpu.CompilerParams(
            collective_id=0, has_side_effects=True, vmem_limit_bytes=60 << 20
        ),
    )(owners, locals_, queries, companies)


def gather_rows(hot, values):
    total = None
    for _ in range(3):
        head = values.astype(jnp.bfloat16)
        term = jnp.dot(hot, head, preferred_element_type=jnp.float32)
        total = term if total is None else total + term
        values = values - head.astype(jnp.float32)
    return total


def finish_kernel(recv_ref, slot_ref, rel_ref, prob_ref):
    lane = lax.broadcasted_iota(jnp.int32, (REQ, 128), 1)
    slots = slot_ref[...]
    hot_row = jnp.where(lane == slots[:, 0:1], 1.0, 0.0).astype(jnp.bfloat16)
    picked = gather_rows(hot_row, recv_ref[...].reshape(128, 128))
    score = jnp.sum(jnp.where(lane == slots[:, 64:65], picked, 0.0), axis=1, keepdims=True)
    step = lax.broadcasted_iota(jnp.int32, (ARTS * PER, 128), 0)
    wide = lax.broadcasted_iota(jnp.int32, (ARTS * PER, 128), 1)
    table = jnp.zeros((ARTS * PER, 128), jnp.float32)
    for r in range(ROWS):
        mine = score[r * ARTS * PER : (r + 1) * ARTS * PER]
        table = jnp.where(wide == r * PER + (step & 3), mine, table)
    table = jnp.sum(table.reshape(ARTS, PER, 128), axis=1)[:, 0:NC]
    relevance = table - jnp.sum(table, axis=1, keepdims=True) * (1.0 / NC)
    weights = jnp.exp(TEMPER * relevance)
    probs = weights / jnp.sum(weights, axis=1, keepdims=True)
    rel_ref[...] = relevance
    prob_ref[...] = probs


def finish(part, slots):
    return pl.pallas_call(
        finish_kernel,
        out_shape=(jax.ShapeDtypeStruct((ARTS, NC), jnp.float32),) * 2,
        in_specs=[VMEM, VMEM],
        out_specs=(VMEM, VMEM),
    )(part, slots)


def per_device(queries, cand_owner, cand_local, companies):
    held = queries.reshape(ARTS, LQ, E)
    owners = jnp.transpose(cand_owner, (0, 2, 1))
    locals_ = jnp.transpose(cand_local, (0, 2, 1))
    return finish(*meet(owners, locals_, held, companies))


def solution(mesh):
    placed = (
        P("art", "seq", None, None),
        P(("art", "seq"), None, None),
        P(("art", "seq"), None, None),
        P("art", None, None),
    )
    return jax.shard_map(
        per_device,
        mesh=mesh,
        in_specs=placed,
        out_specs=(P(("art", "seq"), None), P(("art", "seq"), None)),
        check_vma=False,
    )
```

```python
import math

import jax
import jax.numpy as jnp
from jax import lax
from jax.experimental import pallas as pl
from jax.experimental.pallas import tpu as pltpu
from jax.sharding import PartitionSpec as P

EPS = 1e-06
SHARP = 16.0
TEMPER = 4.0
MESH = pl.DeviceIdType.MESH
HBM = pl.BlockSpec(memory_space=pl.ANY)
VMEM = pl.BlockSpec(memory_space=pltpu.VMEM)

NX, NY, NZ = 4, 4, 8
ARTS = 12
PART = ARTS // NX
LQ, LC, E = 256, 64, 128
NC = 64
ROWS, PER = 16, 4
C_DEV = 256
CAP = 18
GROUP = 6
GROUPS = CAP // GROUP
WORKERS = NZ * 2
REQ = ARTS * NC
SPLIT = 160
QUARTER = SPLIT // NX
HALF = QUARTER // 2
REST = (C_DEV - SPLIT) // 2
RING = (0, 7, 1, 6, 2, 5, 3, 4)
SPOT = {dz: i for i, dz in enumerate(RING)}
NEAR = 5
N_COPIES = 112


def unit(values):
    wide = values.astype(jnp.float32)
    return wide * lax.rsqrt(jnp.sum(wide * wide, axis=-1, keepdims=True) + EPS)


def place():
    art, x = lax.axis_index("art"), lax.axis_index("seq")
    return art // (NY * 2), (art // 2) % NY, art % 2, x


def build(own_ref, loc_ref, list_ref, slot_ref):
    z, y, c, x = place()
    owner = own_ref[...].reshape(ARTS * PER, ROWS)
    local = loc_ref[...].reshape(ARTS * PER, ROWS)
    oz, oy, oc = owner >> 3, (owner >> 1) & 3, owner & 1
    dz = (z - oz) & (NZ - 1)
    ring = jnp.where(dz < NZ // 2, 2 * dz, 2 * (NZ - dz) - 1)
    side = ring * 2 + ((oc + c) & 1)
    packed = (((side * 4 + ((oy - y) & 3)) * 64 + (oz * 2 + oc) * NY + oy) * 256) + local
    packed = jnp.concatenate([packed[:, r : r + 1] for r in range(ROWS)], axis=0)
    lane = lax.broadcasted_iota(jnp.int32, (REQ, 128), 1)
    wide = jnp.broadcast_to(packed, (REQ, 128))
    hot = lane == ((wide >> 8) & 63)
    marks = jnp.where(hot, 1.0, 0.0)
    table = marks.astype(jnp.bfloat16)
    first = lax.broadcasted_iota(jnp.int32, (128, 128), 0)
    second = lax.broadcasted_iota(jnp.int32, (128, 128), 1)
    before = jnp.where(second < first, 1.0, 0.0).astype(jnp.bfloat16)
    seen = jnp.zeros((1, 128), jnp.float32)
    ranks = []
    for i in range(REQ // 128):
        some = slice(i * 128, (i + 1) * 128)
        counts = jnp.dot(before, table[some], preferred_element_type=jnp.float32) + seen
        ranks.append(jnp.sum(jnp.where(hot[some], counts, 0.0), axis=1, keepdims=True))
        seen = seen + jnp.sum(marks[some], axis=0, keepdims=True)
    rank = jnp.broadcast_to(jnp.concatenate(ranks, axis=0).astype(jnp.int32), (REQ, 128))
    step = lax.broadcasted_iota(jnp.int32, (ARTS * PER, 128), 0)
    article = step >> 2
    spot = ((x - article) & 3) * PART + (article >> 2)
    spot = jnp.concatenate([spot] * ROWS, axis=0)
    value = jnp.where(lane < 64, spot, wide & 255)
    entry = jnp.where((lane & 63) == rank, value, 0).astype(jnp.float32).astype(jnp.bfloat16)
    lists = lax.dot_general(table, entry, (((0,), (0,)), ((), ())), preferred_element_type=jnp.float32)
    lists = lists[: WORKERS * NY].astype(jnp.int32)
    for w in range(WORKERS):
        list_ref[w, 0:NY] = lists[w * NY : (w + 1) * NY]
        list_ref[w, NY:8] = jnp.zeros((8 - NY, 128), jnp.int32)
    line = (rank * 43) >> 8
    slots = jnp.where(
        lane < 64, (wide >> 16) * 8 + rank - line * GROUP, ((wide >> 14) & 3) * GROUPS + line
    )
    slot_ref[...] = slots.astype(jnp.float32).astype(jnp.bfloat16)


def meet_kernel(
    own_ref, loc_ref, q_hbm, c_hbm, back_ref, slot_hbm,
    raw_ref, qt_ref, near_ref, far_ref, cat0, cat1, cat2, cat3,
    slot_ref, list_ref, lrecv_ref, lists, part_ref, send_sem, recv_sem, local_sem,
):
    slabs = (cat1, cat2, cat3)
    z, y, c, x = place()

    def at(dz=0, dy=0, dc=0, dx=0):
        zz, yy, cc, xx = (z + dz + NZ) % NZ, (y + dy + NY) % NY, (c + dc) % 2, (x + dx + NX) % NX
        return ((zz * NY + yy) * 2 + cc, xx)

    peers = [at(dz=-d, dc=k) for d in range(NZ) for k in range(2) if d or k]
    peers += [at(dy=1), at(dy=-1), at(dx=1), at(dx=2), at(dx=3)]
    barrier = pltpu.get_barrier_semaphore()
    for peer in peers:
        pl.semaphore_signal(barrier, inc=1, device_id=peer, device_id_type=MESH)

    def load(src, dst, n):
        copy = pltpu.make_async_copy(src, dst, local_sem.at[n])
        copy.start()
        return copy

    def quarter(of, h):
        return pl.ds(((x + of + NX) % NX) * QUARTER + h * HALF, HALF)

    def rest(h):
        return pl.ds(SPLIT + h * REST, REST)

    whole = [pl.ds(((x + of) % NX) * QUARTER, QUARTER) for of in range(NX)]
    tail = pl.ds(SPLIT, C_DEV - SPLIT)
    in_first = load(c_hbm.at[whole[0]], cat0.at[whole[0]], 0)
    in_query = load(q_hbm, raw_ref, 1)
    in_tail = load(c_hbm.at[tail], cat0.at[tail], 2)
    in_other = [load(c_hbm.at[whole[of]], cat0.at[whole[of]], 2 + of) for of in (1, 2, 3)]

    def normalise(start, count):
        def some(i, carry):
            rows = pl.ds(start + i * 8, 8)
            cat0[rows] = unit(cat0[rows]).astype(jnp.bfloat16)
            return carry

        lax.fori_loop(0, count // 8, some, 0)

    in_first.wait()
    normalise(x * QUARTER, QUARTER)
    in_query.wait()
    for a in range(ARTS):
        qt_ref[a] = jnp.transpose(unit(raw_ref[a])).astype(jnp.bfloat16)
    for m in range(PART):
        near_ref[0, 0, m] = qt_ref[x * PART + m]
    pl.semaphore_wait(barrier, len(peers))

    copies = {}

    def send(name, src, dst, device):
        assert name not in copies
        n = len(copies)
        copy = pltpu.make_async_remote_copy(
            src_ref=src,
            dst_ref=dst,
            send_sem=send_sem.at[n],
            recv_sem=recv_sem.at[n],
            device_id=device,
            device_id_type=MESH,
        )
        copies[name] = copy
        copy.start()

    received = set()

    def got(*names):
        for name in names:
            if name not in received:
                received.add(name)
                copies[name].wait_recv()

    def tile(dz, k):
        i = SPOT[dz]
        return near_ref.at[i, k] if i < NEAR else far_ref.at[i - NEAR, k]

    def z_first(j):
        rows = pl.ds(j * PART, PART)
        src = tile(0, 0).at[rows]
        send(f"p1{j}", src, tile(NZ - 1, 0).at[rows], at(dz=1))
        send(f"m1{j}", src, tile(1, 0).at[rows], at(dz=-1))

    def z_next(step, half, both=(True, True)):
        rows = pl.ds(half * 2 * PART, 2 * PART)
        if both[0]:
            send(f"p{step}{half}", tile(NZ - step + 1, 0).at[rows], tile(NZ - step, 0).at[rows], at(dz=1))
        if both[1]:
            send(f"m{step}{half}", tile(step - 1, 0).at[rows], tile(step, 0).at[rows], at(dz=-1))

    def partner(dz):
        send(f"c{dz}", tile(dz, 0), tile(dz, 1), at(dc=1))

    def y_up(tag, rows, h):
        send(f"up{tag}{h}", cat0.at[rows(h)], slabs[2].at[rows(h)], at(dy=1))

    def y_down(tag, rows, h):
        send(f"dn{tag}{h}", cat0.at[rows(h)], slabs[0].at[rows(h)], at(dy=-1))

    def y_fwd(tag, rows):
        send(f"upf{tag}", slabs[2].at[rows(0)], slabs[1].at[rows(0)], at(dy=1))
        send(f"dnf{tag}", slabs[0].at[rows(1)], slabs[1].at[rows(1)], at(dy=-1))

    def x_own(d, h):
        rows = quarter(0, h)
        send(f"xp{d}{h}", slabs[d].at[rows], slabs[d].at[rows], at(dx=1))
        send(f"xm{d}{h}", slabs[d].at[rows], slabs[d].at[rows], at(dx=-1))

    def x_fwd(d):
        got(f"xp{d}0")
        rows = quarter(-1, 0)
        send(f"xpf{d}", slabs[d].at[rows], slabs[d].at[rows], at(dx=1))
        got(f"xm{d}1")
        rows = quarter(1, 1)
        send(f"xmf{d}", slabs[d].at[rows], slabs[d].at[rows], at(dx=-1))

    def mine(h):
        return quarter(0, h)

    y_up("s", mine, 0)
    y_down("s", mine, 1)
    y_up("s", mine, 1)
    y_down("s", mine, 0)
    for j in (1, 3, 2):
        send(
            f"e{j}",
            qt_ref.at[pl.ds(((x + j) % NX) * PART, PART)],
            tile(0, 0).at[pl.ds(j * PART, PART)],
            at(dx=j),
        )
    z_first(0)
    in_tail.wait()
    normalise(SPLIT, C_DEV - SPLIT)
    got("e1")
    z_first(1)
    got("e3")
    z_first(3)
    build(own_ref, loc_ref, list_ref, slot_ref)
    got("ups0", "dns1")
    y_fwd("s", mine)
    for h in (0, 1):
        y_up("r", rest, h)
        y_down("r", rest, 1 - h)
    x_own(2, 0)
    x_own(0, 1)
    got("e2")
    z_first(2)
    partner(0)
    got("p10", "p11", "m10", "m11")
    z_next(2, 0)
    own_list = load(list_ref.at[z * 2 + c], lrecv_ref.at[0], 0)
    for d in range(NZ):
        for k in range(2):
            if d or k:
                worker = ((z - d + NZ) % NZ) * 2 + (c + k) % 2
                send(f"l{d}{k}", list_ref.at[worker], lrecv_ref.at[SPOT[d] * 2 + k], at(dz=-d, dc=k))
    got("ups1", "dns0")
    x_own(2, 1)
    x_own(0, 0)
    got("p12", "p13", "m12", "m13")
    z_next(2, 1)
    partner(NZ - 1)
    partner(1)
    got("upfs", "dnfs")
    x_own(1, 0)
    x_own(1, 1)
    own_list.wait()
    got(*[n for n in copies if n[0] == "l"])
    lists_in = load(lrecv_ref, lists, 0)
    for of in (1, 2, 3):
        in_other[of - 1].wait()
        normalise(((x + of) % NX) * QUARTER, QUARTER)
    got("p20", "m20")
    z_next(3, 0)
    x_fwd(2)
    x_fwd(0)
    got("p21", "m21")
    z_next(3, 1)
    partner(NZ - 2)
    partner(2)
    got("upr0", "dnr1")
    y_fwd("r", rest)
    lists_in.wait()

    lane = lax.broadcasted_iota(jnp.int32, (8, 128), 1)
    cats = (cat0, cat1, cat2, cat3)

    def score(d, queries, i, base):
        owner = (y + d) % NY
        for k in range(2):
            w = (base + i) * 2 + k
            scores = jnp.zeros((8, 128), jnp.float32) if d == 0 else part_ref[w]
            for g in range(GROUPS):
                rows = []
                for u in range(GROUP):
                    slot = g * GROUP + u
                    query = queries[i, k, jnp.minimum(lists[w, owner, slot] & 15, ARTS - 1)]
                    block = cats[d][lists[w, owner, 64 + slot] & (C_DEV - 1)]
                    sims = jnp.dot(block, query, preferred_element_type=jnp.float32)
                    mass = jnp.exp2(sims * (SHARP * math.log2(math.e)))
                    rows.append(jnp.sum(jnp.sum(mass.reshape(8, 8, LQ), axis=0), axis=0, keepdims=True))
                rows += [jnp.ones((8 - GROUP, LQ), jnp.float32)]
                logs = jnp.log(jnp.concatenate(rows, axis=0))
                total = jnp.sum(logs, axis=1, keepdims=True) * (1.0 / SHARP)
                scores = jnp.where(lane == d * GROUPS + g, total, scores)
            part_ref[w] = scores

    def wave(d, far):
        queries, base, count = (far_ref, NEAR, NZ - NEAR) if far else (near_ref, 0, NEAR)

        def body(i, carry):
            score(d, queries, i, base)
            return carry

        lax.fori_loop(0, count, body, 0, unroll=(d == 2))

    slots_out = load(slot_ref, slot_hbm, 1)
    got("c0", "c1", f"c{NZ - 1}", "c2", f"c{NZ - 2}")
    wave(0, False)
    got("p30")
    z_next(4, 0, (True, False))
    x_fwd(1)
    got("m30", "m31")
    z_next(4, 1, (False, True))
    got("p31")
    partner(NZ - 3)
    partner(3)
    got("ups0", "ups1", "upr0", "upr1", "xp20", "xp21", "xm20", "xm21", "xpf2", "xmf2")
    wave(3, False)
    got("p40", "m41")
    partner(4)
    got(*[n for n in copies if n[0] == "c"])
    wave(0, True)
    wave(3, True)
    got("dns0", "dns1", "dnr0", "dnr1", "xp00", "xp01", "xm00", "xm01", "xpf0", "xmf0")
    wave(1, False)
    wave(1, True)
    for name in list(copies):
        got(name)

    def back(i):
        for k in range(2):
            d, n = RING[i], i * 2 + k
            if d or k:
                send(f"b{d}{k}", part_ref.at[n], back_ref.at[n], at(dz=d, dc=k))

    wave(2, True)
    for i in range(NZ - 1, NEAR - 1, -1):
        back(i)
    wave(2, False)
    for i in range(NEAR - 1, -1, -1):
        back(i)
    own_part = load(part_ref.at[0], back_ref.at[0], 0)
    own_part.wait()
    slots_out.wait()
    for name in list(copies):
        got(name)
    for copy in copies.values():
        copy.wait_send()


def meet(owners, locals_, queries, companies):
    return pl.pallas_call(
        meet_kernel,
        out_shape=(
            jax.ShapeDtypeStruct((WORKERS, 8, 128), jnp.float32),
            jax.ShapeDtypeStruct((REQ, 128), jnp.bfloat16),
        ),
        in_specs=[VMEM, VMEM, HBM, HBM],
        out_specs=(VMEM, HBM),
        scratch_shapes=[
            pltpu.VMEM((ARTS, LQ, E), jnp.bfloat16),
            pltpu.VMEM((ARTS, E, LQ), jnp.bfloat16),
            pltpu.VMEM((NEAR, 2, ARTS, E, LQ), jnp.bfloat16),
            pltpu.VMEM((NZ - NEAR, 2, ARTS, E, LQ), jnp.bfloat16),
        ]
        + [pltpu.VMEM((C_DEV, LC, E), jnp.bfloat16)] * NY
        + [
            pltpu.VMEM((REQ, 128), jnp.bfloat16),
            pltpu.VMEM((WORKERS, 8, 128), jnp.int32),
            pltpu.VMEM((WORKERS, 8, 128), jnp.int32),
            pltpu.SMEM((WORKERS, 8, 128), jnp.int32),
            pltpu.VMEM((WORKERS, 8, 128), jnp.float32),
            pltpu.SemaphoreType.DMA((N_COPIES,)),
            pltpu.SemaphoreType.DMA((N_COPIES,)),
            pltpu.SemaphoreType.DMA((6,)),
        ],
        compiler_params=pltpu.CompilerParams(
            collective_id=0, has_side_effects=True, vmem_limit_bytes=60 << 20
        ),
    )(owners, locals_, queries, companies)


def gather_rows(hot, values):
    total = None
    for _ in range(3):
        head = values.astype(jnp.bfloat16)
        term = jnp.dot(hot, head, preferred_element_type=jnp.float32)
        total = term if total is None else total + term
        values = values - head.astype(jnp.float32)
    return total


def finish_kernel(recv_ref, slot_ref, rel_ref, prob_ref):
    lane = lax.broadcasted_iota(jnp.int32, (REQ, 128), 1)
    slots = slot_ref[...].astype(jnp.float32).astype(jnp.int32)
    hot_row = jnp.where(lane == slots[:, 0:1], 1.0, 0.0).astype(jnp.bfloat16)
    picked = gather_rows(hot_row, recv_ref[...].reshape(128, 128))
    score = jnp.sum(jnp.where(lane == slots[:, 64:65], picked, 0.0), axis=1, keepdims=True)
    step = lax.broadcasted_iota(jnp.int32, (ARTS * PER, 128), 0)
    wide = lax.broadcasted_iota(jnp.int32, (ARTS * PER, 128), 1)
    table = jnp.zeros((ARTS * PER, 128), jnp.float32)
    for r in range(ROWS):
        mine = score[r * ARTS * PER : (r + 1) * ARTS * PER]
        table = jnp.where(wide == r * PER + (step & 3), mine, table)
    table = jnp.sum(table.reshape(ARTS, PER, 128), axis=1)[:, 0:NC]
    relevance = table - jnp.sum(table, axis=1, keepdims=True) * (1.0 / NC)
    weights = jnp.exp(TEMPER * relevance)
    probs = weights / jnp.sum(weights, axis=1, keepdims=True)
    rel_ref[...] = relevance
    prob_ref[...] = probs


def finish(part, slots):
    return pl.pallas_call(
        finish_kernel,
        out_shape=(jax.ShapeDtypeStruct((ARTS, NC), jnp.float32),) * 2,
        in_specs=[VMEM, VMEM],
        out_specs=(VMEM, VMEM),
    )(part, slots)


def per_device(queries, cand_owner, cand_local, companies):
    held = queries.reshape(ARTS, LQ, E)
    owners = jnp.transpose(cand_owner, (0, 2, 1))
    locals_ = jnp.transpose(cand_local, (0, 2, 1))
    return finish(*meet(owners, locals_, held, companies))


def solution(mesh):
    placed = (
        P("art", "seq", None, None),
        P(("art", "seq"), None, None),
        P(("art", "seq"), None, None),
        P("art", None, None),
    )
    return jax.shard_map(
        per_device,
        mesh=mesh,
        in_specs=placed,
        out_specs=(P(("art", "seq"), None), P(("art", "seq"), None)),
        check_vma=False,
    )
```
